128 devices in a mesh: ctx: 32 (over z_hi, x, y), grp: 4 (over z_lo, core).
Axes of the slice: x: 4, y: 4, z: 4 (z_hi: 2, z_lo: 2; z = z_hi * 2 + z_lo), core: 2. Of those that a mesh axis runs over, the one named last changes fastest.
Arguments:
- queries: bfloat16 [32768, 1024], P(('ctx', 'grp')), may hold values from -360 to 360
- key_rows: bfloat16 [32768, 256], P(('ctx', 'grp')), may hold values from -6 to 6
- value_rows: bfloat16 [32768, 256], P(('ctx', 'grp')), may hold values from -6 to 6
- chosen_offset: int32 [128, 4], replicated, may hold values from 2 to 8, as said below
- chosen_count: int32 [128], replicated, may hold values from 0 to 4, as said below
- head_gain: float32 [1024], replicated, may hold values from 0.25 to 1.75
- cotangent: bfloat16 [32768, 1024], P(('ctx', 'grp')), may hold values from -6 to 6
Outputs:
- outputs: bfloat16 [32768, 1024], P(('ctx', 'grp'))
- grad_queries: bfloat16 [32768, 1024], P(('ctx', 'grp'))
- grad_keys: bfloat16 [32768, 256], P(('ctx', 'grp'))
- grad_values: bfloat16 [32768, 256], P(('ctx', 'grp'))
The draws below stay inside these ranges and needn't reach their ends.
Inputs may be any that keep to these rules, and one draw needn't show every extreme that they name: `chosen_offset`: within a block's row the 4 offsets are distinct. `chosen_count`: slots at or after a block's count are unused.
All inputs are finite; a program needn't handle non-finite values.
Results may differ from the reference program's by a relative error of at most 0.0059.
Values may be sent and summed in bfloat16 or wider, within the bound.
No kernel may reach another device: no remote copies, remote signals or barrier semaphores. Data moves between devices by JAX's collectives and lax.ppermute only.
A program may use at most 64 MiB of HBM per device.

```python
import jax
import jax.numpy as jnp
from jax import lax

TOK_DEV = 256
QUERY_HEADS = 8
KEY_VALUE_HEADS = 2
HEAD_SIZE = 128
SEL = 4
LOOK = 8
NBLK = 128
SEQUENCE_TOKENS = 32768
QW = 1024
KW = 256


def selection_tables(key):
    base = jax.random.fold_in(key, 21)
    ranks = jax.random.randint(jax.random.fold_in(base, 1), (NBLK, LOOK - 1), 0, 4096) * 8
    ranks = ranks + jnp.arange(LOOK - 1)[None, :]
    order = jnp.argsort(ranks, axis=1, stable=True)
    offsets = (order[:, :SEL] + 2).astype(jnp.int32)
    fixed_row = jnp.concatenate([jnp.array([LOOK]), jnp.arange(2, SEL + 1)]).astype(jnp.int32)
    offsets = offsets.at[NBLK - 1].set(fixed_row)
    counts = jax.random.randint(jax.random.fold_in(base, 2), (NBLK,), 0, SEL + 1).astype(jnp.int32)
    counts = counts.at[NBLK - 1].set(SEL).at[NBLK - 2].set(0)
    return (offsets, counts)


def key_table(key):
    drawn = jax.random.normal(jax.random.fold_in(key, 31), (SEQUENCE_TOKENS, KW), jnp.float32)
    return jnp.clip(drawn, -6.0, 6.0)


def draw_key_rows(key, part):
    return key_table(key).astype(jnp.bfloat16)


def draw_chosen_offset(key, part):
    return selection_tables(key)[0]


def draw_chosen_count(key, part):
    return selection_tables(key)[1]


def draw_queries(key, part):
    drawn = jnp.clip(jax.random.normal(jax.random.fold_in(key, 41), (SEQUENCE_TOKENS, QW), jnp.float32), -6.0, 6.0)
    return drawn.astype(jnp.bfloat16)


def steps_of(rng, shape, cuts, low, top_value):
    factor_of, own = 1.0, jax.random.fold_in(rng, 6)
    for axis_at, parts in cuts:
        draws = jnp.exp(jax.random.uniform(jax.random.fold_in(own, axis_at), (parts,), jnp.float32, low / len(cuts), top_value / len(cuts)))
        factor_of = factor_of * jnp.repeat(draws, shape[axis_at] // parts).reshape([-1 if axis == axis_at else 1 for axis in range(len(shape))])
    return factor_of


def gaussian(stream_key, dims, scale, reach, pieces=(), held_as=jnp.bfloat16):
    gain = steps_of(stream_key, dims, pieces, -0.22, 0.18) if pieces else 1.0
    values = jax.random.normal(stream_key, dims, jnp.float32) * scale * gain
    return jnp.minimum(jnp.maximum(values, -reach), reach).astype(held_as)


def setup_inputs(seed: int = 0) -> dict:
    arg_keys = jax.random.split(jax.random.key(seed), 8)
    return {
        "queries": draw_queries(jax.random.fold_in(arg_keys[7], 71), 0),
        "key_rows": draw_key_rows(jax.random.fold_in(arg_keys[7], 71), 0),
        "value_rows": gaussian(arg_keys[2], (SEQUENCE_TOKENS, KW), 1.0, 6.0, ((0, 128),)),
        "chosen_offset": draw_chosen_offset(jax.random.fold_in(arg_keys[7], 71), 0),
        "chosen_count": draw_chosen_count(jax.random.fold_in(arg_keys[7], 71), 0),
        "head_gain": jnp.clip(1.0 + 0.15 * jax.random.normal(arg_keys[5], (QW,), jnp.float32), 0.25, 1.75),
        "cotangent": gaussian(arg_keys[6], (SEQUENCE_TOKENS, QW), 1.0, 6.0, ((0, 128),)),
    }


masked_value = -1e+30
norm_epsilon = 1e-06

def attend(query_head, branch_keys, branch_values, branch_mask):
    score_scale = query_head.shape[-1] ** (-0.5)
    scores = score_scale * jnp.dot(query_head, branch_keys.T, preferred_element_type=jnp.float32)
    masked = jnp.where(branch_mask, scores, masked_value)
    row_max = lax.optimization_barrier(jnp.max(masked, axis=-1, keepdims=True))
    expd = jnp.where(branch_mask, jnp.exp(masked - row_max), 0.0)
    row_total = lax.optimization_barrier(jnp.sum(expd, axis=-1, keepdims=True))
    soft_weights = expd / jnp.maximum(row_total, 1.0)
    low_weights = soft_weights.astype(jnp.bfloat16)
    branch_out = jnp.dot(low_weights, branch_values, preferred_element_type=jnp.float32)
    return (branch_out, soft_weights, low_weights)

def attend_back(query_head, branch_keys, branch_values, soft_weights, low_weights, grad_low):
    score_scale = query_head.shape[-1] ** (-0.5)
    grad_vals = jnp.dot(low_weights.T, grad_low, preferred_element_type=jnp.float32)
    grad_weights = jnp.dot(grad_low, branch_values.T, preferred_element_type=jnp.float32)
    row_inner = lax.optimization_barrier(jnp.sum(soft_weights * grad_weights, axis=-1, keepdims=True))
    grad_scores = (score_scale * soft_weights * (grad_weights - row_inner)).astype(jnp.bfloat16)
    grad_query = jnp.dot(grad_scores, branch_keys, preferred_element_type=jnp.float32)
    grad_keys = jnp.dot(grad_scores.T, query_head, preferred_element_type=jnp.float32)
    return (grad_query, grad_keys, grad_vals)

def block_pass(queries_blk, window_token_rows, selected_block_rows, window_mask, chosen_mask, grad_blk, head_gain):
    group_length = QUERY_HEADS // KEY_VALUE_HEADS
    out_list = []
    gradq_list = []
    window_pieces = [jnp.zeros((window_token_rows.shape[0], HEAD_SIZE), jnp.float32)] * (2 * KEY_VALUE_HEADS)
    selected_pieces = [jnp.zeros((selected_block_rows.shape[0], HEAD_SIZE), jnp.float32)] * (2 * KEY_VALUE_HEADS)
    for head_index in range(QUERY_HEADS):
        group_position = head_index // group_length
        qcols = slice(head_index * HEAD_SIZE, (head_index + 1) * HEAD_SIZE)
        kcols = slice(group_position * HEAD_SIZE, (group_position + 1) * HEAD_SIZE)
        value_columns = slice((KEY_VALUE_HEADS + group_position) * HEAD_SIZE, (KEY_VALUE_HEADS + group_position + 1) * HEAD_SIZE)
        query_head = queries_blk[:, qcols]
        gain_head = head_gain[qcols]
        out_w, soft_w, low_w = attend(query_head, window_token_rows[:, kcols], window_token_rows[:, value_columns], window_mask)
        out_c, soft_c, low_c = attend(query_head, selected_block_rows[:, kcols], selected_block_rows[:, value_columns], chosen_mask)
        summed = out_w + out_c
        inverse = lax.rsqrt(lax.optimization_barrier(jnp.mean(summed * summed, axis=-1, keepdims=True)) + norm_epsilon)
        normed = summed * inverse
        out_list.append((normed * gain_head).astype(jnp.bfloat16))
        grad_normed = grad_blk[:, qcols].astype(jnp.float32) * gain_head
        grad_summed = inverse * (grad_normed - normed * lax.optimization_barrier(jnp.mean(grad_normed * normed, axis=-1, keepdims=True)))
        grad_low = grad_summed.astype(jnp.bfloat16)
        gq_w, gk_w, grad_value_window = attend_back(query_head, window_token_rows[:, kcols], window_token_rows[:, value_columns], soft_w, low_w, grad_low)
        gq_c, gk_c, grad_value_selected = attend_back(query_head, selected_block_rows[:, kcols], selected_block_rows[:, value_columns], soft_c, low_c, grad_low)
        gradq_list.append((gq_w + gq_c).astype(jnp.bfloat16))
        window_pieces[group_position] = window_pieces[group_position] + gk_w
        window_pieces[KEY_VALUE_HEADS + group_position] = window_pieces[KEY_VALUE_HEADS + group_position] + grad_value_window
        selected_pieces[group_position] = selected_pieces[group_position] + gk_c
        selected_pieces[KEY_VALUE_HEADS + group_position] = selected_pieces[KEY_VALUE_HEADS + group_position] + grad_value_selected
    return (jnp.concatenate(out_list, axis=1), jnp.concatenate(gradq_list, axis=1), jnp.concatenate(window_pieces, axis=1), jnp.concatenate(selected_pieces, axis=1))

def reference(queries, key_rows, value_rows, chosen_offset, chosen_count, head_gain, cotangent):
    kv_width = 2 * KW
    kv_table = jnp.concatenate([key_rows, value_rows], axis=1).reshape(NBLK, TOK_DEV, kv_width)
    query_table = queries.reshape(NBLK, TOK_DEV, QW)
    grad_table = cotangent.reshape(NBLK, TOK_DEV, QW)
    causal = jnp.arange(TOK_DEV)[:, None] >= jnp.arange(TOK_DEV)[None, :]

    def one_block(moving, block_index):
        own_block = kv_table[block_index]
        prev_index = jnp.maximum(block_index - 1, 0)
        previous = kv_table[prev_index]
        offsets = chosen_offset[block_index]
        counts = chosen_count[block_index]
        sources = block_index - offsets
        slot_valid = (jnp.arange(SEL) < counts) & (sources >= 0)
        safe_sources = jnp.maximum(sources, 0)
        selected_block_rows = kv_table[safe_sources].reshape(SEL * TOK_DEV, kv_width)
        window_token_rows = jnp.concatenate([own_block, previous], axis=0)
        window_mask = jnp.concatenate([causal, jnp.broadcast_to(block_index >= 1, (TOK_DEV, TOK_DEV))], axis=1)
        chosen_mask = jnp.repeat(slot_valid, TOK_DEV)[None, :]
        out_blk, gradq_blk, grad_window, grad_chosen = block_pass(query_table[block_index], window_token_rows, selected_block_rows, window_mask, chosen_mask, grad_table[block_index], head_gain)
        moving = moving.at[block_index].add(grad_window[:TOK_DEV])
        moving = moving.at[prev_index].add(grad_window[TOK_DEV:])
        moving = moving.at[safe_sources].add(grad_chosen.reshape(SEL, TOK_DEV, kv_width))
        return (moving, (out_blk, gradq_blk))
    start = jnp.zeros((NBLK, TOK_DEV, kv_width), jnp.float32)
    grad_kv, (out_all, gradq_all) = lax.scan(one_block, start, jnp.arange(NBLK).astype(jnp.int32))
    grad_kv = grad_kv.reshape(SEQUENCE_TOKENS, kv_width)
    return (out_all.reshape(SEQUENCE_TOKENS, QW), gradq_all.reshape(SEQUENCE_TOKENS, QW), grad_kv[:, :KW].astype(jnp.bfloat16), grad_kv[:, KW:].astype(jnp.bfloat16))
```

```python
import math

import jax
import jax.numpy as jnp
from jax import lax
from jax.experimental import pallas as pl
from jax.experimental.pallas import tpu as pltpu
from jax.sharding import PartitionSpec as P

AXES = ("ctx", "grp")
ROWS = 256
HEAD = 128
GROUP = 4
HALF = GROUP * HEAD
COLS = GROUP * ROWS
SEL = 4
SHIFTS = 4
TABLE = 2 * (SHIFTS + 1)
SCALE = HEAD**-0.5
SCALE_LOG2E = SCALE * math.log2(math.e)
MASKED = -1e30
EPS = 1e-06

NT = (((1,), (1,)), ((), ()))
NN = (((1,), (0,)), ((), ()))


def dot(a, b, dims):
    return lax.dot_general(a, b, dims, preferred_element_type=jnp.float32)


def attention_kernel(
    where_ref,
    offset_ref,
    count_ref,
    q0_ref,
    q1_ref,
    ct0_ref,
    ct1_ref,
    gain_ref,
    kv0_ref,
    kv1_ref,
    kv2_ref,
    kv3_ref,
    kv4_ref,
    out_ref,
    gq_ref,
    own_ref,
    g1_ref,
    g2_ref,
    g3_ref,
    g4_ref,
    table,
    soft,
    acc,
    qs,
    gain_t,
    ot,
    gqt,
):
    me = where_ref[0]
    half = me % 2
    chip = me // 2

    for k, ref in enumerate((kv0_ref, kv1_ref, kv2_ref, kv3_ref, kv4_ref)):
        for s in range(2):
            table[2 * k + s] = ref[s]
    acc[...] = jnp.zeros_like(acc)
    gains = gain_ref[pl.ds(half, 1), :]
    for n in range(GROUP):
        row = gains[:, n * HEAD : (n + 1) * HEAD]
        gain_t[:, n * ROWS : (n + 1) * ROWS] = jnp.broadcast_to(row, (ROWS, HEAD)).T

    def place(block):
        return 2 * (chip - block // 2) + (block % 2 + half) % 2

    for i, (q_ref, ct_ref) in enumerate(((q0_ref, ct0_ref), (q1_ref, ct1_ref))):
        block = me if i == 0 else me + 1 - 2 * half
        for n in range(GROUP):
            qs[n * ROWS : (n + 1) * ROWS, :] = q_ref[:, n * HEAD : (n + 1) * HEAD]
        count = count_ref[block]
        prev_seen = block >= 1

        def slot_of(j):
            source = block - offset_ref[block * SEL + j]
            return source >= 0, place(jnp.maximum(source, 0))

        def scores(at):
            return dot(table[at, :, :HEAD], qs[...], NT)

        low = jnp.full((1, COLS), MASKED, jnp.float32)
        zero = jnp.zeros((1, COLS), jnp.float32)

        diag = scores(place(block))
        key_at = lax.broadcasted_iota(jnp.int32, (ROWS, COLS), 0)
        query_at = lax.broadcasted_iota(jnp.int32, (ROWS, COLS), 1) % ROWS
        diag = jnp.where(key_at <= query_at, diag, MASKED)
        soft[0] = diag
        top_w = jnp.max(diag, axis=0, keepdims=True)

        def prev_scores(top):
            s = scores(place(block - 1))
            soft[1] = s
            return jnp.maximum(top, jnp.max(s, axis=0, keepdims=True))

        top_w = lax.cond(prev_seen, prev_scores, lambda top: top, top_w)

        def chosen_scores(j, top):
            seen, at = slot_of(j)

            def run(top):
                s = scores(at)
                soft[2 + j] = s
                return jnp.maximum(top, jnp.max(s, axis=0, keepdims=True))

            return lax.cond(seen, run, lambda top: top, top)

        top_c = lax.fori_loop(0, count, chosen_scores, low)

        def expo(j, top, total):
            e = jnp.exp2((soft[j] - top) * SCALE_LOG2E)
            soft[j] = e
            return total + jnp.sum(e, axis=0, keepdims=True)

        total_w = expo(0, top_w, zero)
        total_w = lax.cond(prev_seen, lambda t: expo(1, top_w, t), lambda t: t, total_w)

        def chosen_expo(j, total):
            seen, _ = slot_of(j)
            return lax.cond(seen, lambda t: expo(2 + j, top_c, t), lambda t: t, total)

        total_c = lax.fori_loop(0, count, chosen_expo, zero)
        inv_w = 1.0 / jnp.maximum(total_w, 1.0)
        inv_c = 1.0 / jnp.maximum(total_c, 1.0)

        def weigh(j, at, inv, which, first=False):
            p = soft[j] * inv
            soft[j] = p
            part = dot(table[at, :, HEAD:].T, p.astype(jnp.bfloat16), NN)
            if first:
                ot[which] = part
            else:
                ot[which] += part

        weigh(0, place(block), inv_w, 0, True)

        @pl.when(prev_seen)
        def _():
            weigh(1, place(block - 1), inv_w, 0)

        ot[1] = jnp.zeros((HEAD, COLS), jnp.float32)

        def chosen_weigh(j, carry):
            seen, at = slot_of(j)

            @pl.when(seen)
            def _():
                weigh(2 + j, at, inv_c, 1)

            return carry

        lax.fori_loop(0, count, chosen_weigh, 0)

        out_w = ot[0]
        out_c = ot[1]
        summed = out_w + out_c
        inverse = lax.rsqrt(jnp.mean(summed * summed, axis=0, keepdims=True) + EPS)
        normed = summed * inverse
        gain = gain_t[...]
        out_t = normed * gain
        ct_t = jnp.concatenate(
            [
                ct_ref[:, n * HEAD : (n + 1) * HEAD].astype(jnp.float32).T
                for n in range(GROUP)
            ],
            axis=1,
        )
        grad_normed = ct_t * gain
        inner = jnp.mean(grad_normed * normed, axis=0, keepdims=True)
        grad_low = (inverse * (grad_normed - normed * inner)).astype(jnp.bfloat16)
        wide = grad_low.astype(jnp.float32)
        inner_w = jnp.sum(wide * out_w, axis=0, keepdims=True)
        inner_c = jnp.sum(wide * out_c, axis=0, keepdims=True)
        for n in range(GROUP):
            out_ref[i, :, n * HEAD : (n + 1) * HEAD] = out_t[
                :, n * ROWS : (n + 1) * ROWS
            ].T.astype(jnp.bfloat16)

        def back(j, at, inner, first=False):
            p = soft[j]
            grad_w = dot(table[at, :, HEAD:], grad_low, NN)
            grad_s = (SCALE * p * (grad_w - inner)).astype(jnp.bfloat16)
            acc[at, :, HEAD:] += dot(p.astype(jnp.bfloat16), grad_low, NT)
            acc[at, :, :HEAD] += dot(grad_s, qs[...], NN)
            part = dot(table[at, :, :HEAD].T, grad_s, NN)
            if first:
                gqt[...] = part
            else:
                gqt[...] += part

        back(0, place(block), inner_w, True)

        @pl.when(prev_seen)
        def _():
            back(1, place(block - 1), inner_w)

        def chosen_back(j, carry):
            seen, at = slot_of(j)

            @pl.when(seen)
            def _():
                back(2 + j, at, inner_c)

            return carry

        lax.fori_loop(0, count, chosen_back, 0)
        for n in range(GROUP):
            gq_ref[i, :, n * HEAD : (n + 1) * HEAD] = gqt[
                :, n * ROWS : (n + 1) * ROWS
            ].T.astype(jnp.bfloat16)

    own_ref[...] = acc[0:2]
    for k, ref in enumerate((g1_ref, g2_ref, g3_ref, g4_ref)):
        ref[...] = acc[2 * k + 2 : 2 * k + 4].astype(jnp.bfloat16)


def attention(where, offsets, counts, q0, q1, ct0, ct1, gains, *tables):
    vmem = pl.BlockSpec(memory_space=pltpu.VMEM)
    pair = (2, ROWS, 2 * HEAD)
    shapes = (
        jax.ShapeDtypeStruct((2, ROWS, HALF), jnp.bfloat16),
        jax.ShapeDtypeStruct((2, ROWS, HALF), jnp.bfloat16),
        jax.ShapeDtypeStruct(pair, jnp.float32),
    ) + (jax.ShapeDtypeStruct(pair, jnp.bfloat16),) * SHIFTS
    smem = pl.BlockSpec(memory_space=pltpu.SMEM)
    return pl.pallas_call(
        attention_kernel,
        out_shape=shapes,
        in_specs=[smem] * 3 + [vmem] * 10,
        out_specs=[vmem] * 7,
        scratch_shapes=[
            pltpu.VMEM((TABLE, ROWS, 2 * HEAD), jnp.bfloat16),
            pltpu.VMEM((2 + SEL, ROWS, COLS), jnp.float32),
            pltpu.VMEM((TABLE, ROWS, 2 * HEAD), jnp.float32),
            pltpu.VMEM((COLS, HEAD), jnp.bfloat16),
            pltpu.VMEM((HEAD, COLS), jnp.float32),
            pltpu.VMEM((2, HEAD, COLS), jnp.float32),
            pltpu.VMEM((HEAD, COLS), jnp.float32),
        ],
        compiler_params=pltpu.CompilerParams(vmem_limit_bytes=48 << 20),
        cost_estimate=pl.CostEstimate(
            flops=5_000_000_000, bytes_accessed=8_000_000, transcendentals=3_200_000
        ),
        name="attention",
    )(where, offsets, counts, q0, q1, ct0, ct1, gains, *tables)


def per_device(queries, key_rows, value_rows, chosen_offset, chosen_count, head_gain, cotangent):
    size = lax.axis_size(AXES)
    me = lax.axis_index(AXES)
    half = me % 2

    def swap(x):
        return lax.ppermute(x, AXES, [(i, i ^ 1) for i in range(size)])

    def chips_on(x, k):
        return lax.ppermute(x, AXES, [(i, (i + 2 * k) % size) for i in range(size)])

    def part(x, which, width):
        return lax.dynamic_slice(x, (0, which * width), (x.shape[0], width))

    def head_of(which):
        return jnp.concatenate([part(key_rows, which, HEAD), part(value_rows, which, HEAD)], axis=1)

    other = 1 - half
    own = jnp.stack([head_of(half), swap(head_of(other))])
    tables = [own] + [chips_on(own, k) for k in range(1, SHIFTS + 1)]
    q1 = swap(part(queries, other, HALF))
    ct1 = swap(part(cotangent, other, HALF))
    out, gq, grad_own, *grads = attention(
        me.astype(jnp.int32).reshape(1),
        chosen_offset.reshape(-1),
        chosen_count,
        part(queries, half, HALF),
        q1,
        part(cotangent, half, HALF),
        ct1,
        head_gain.reshape(2, HALF),
        *tables,
    )
    total = grad_own
    for k in range(SHIFTS, 0, -1):
        total = total + chips_on(grads[k - 1], -k).astype(jnp.float32)
    total = total.astype(jnp.bfloat16)

    def joined(mine, theirs):
        return jnp.where(
            half == 0,
            jnp.concatenate([mine, theirs], axis=1),
            jnp.concatenate([theirs, mine], axis=1),
        )

    theirs = swap(total[1])
    return (
        joined(out[0], swap(out[1])),
        joined(gq[0], swap(gq[1])),
        joined(total[0, :, :HEAD], theirs[:, :HEAD]),
        joined(total[0, :, HEAD:], theirs[:, HEAD:]),
    )


def solution(mesh):
    rows = P(AXES, None)
    return jax.shard_map(
        per_device,
        mesh=mesh,
        in_specs=(rows, rows, rows, P(), P(), P(), rows),
        out_specs=(rows, rows, rows, rows),
        check_vma=False,
    )
```

```python
import math

import jax
import jax.numpy as jnp
from jax import lax
from jax.experimental import pallas as pl
from jax.experimental.pallas import tpu as pltpu
from jax.sharding import PartitionSpec as P

AXES = ("ctx", "grp")
ROWS = 256
HEAD = 128
GROUP = 4
HALF = GROUP * HEAD
COLS = GROUP * ROWS
SEL = 4
SHIFTS = 4
SCALE = HEAD**-0.5
SCALE_LOG2E = SCALE * math.log2(math.e)
MASKED = -1e30
EPS = 1e-06

NT = (((1,), (1,)), ((), ()))
NN = (((1,), (0,)), ((), ()))
F32 = jnp.float32
BF16 = jnp.bfloat16


def dot(a, b, dims):
    return lax.dot_general(a, b, dims, preferred_element_type=F32)


def geometry(where_ref):
    me = where_ref[0]
    half = me % 2
    chip = me // 2

    def place(block):
        return 2 * (chip - block // 2) + (block % 2 + half) % 2

    return half, (me, me + 1 - 2 * half), place


def stack_heads(qs, q_ref):
    for n in range(GROUP):
        qs[n * ROWS : (n + 1) * ROWS, :] = q_ref[:, n * HEAD : (n + 1) * HEAD]


def window_scores(table, at, before, seen, queries):
    diag = dot(table[at, :, :HEAD], queries, NT)
    key_at = lax.broadcasted_iota(jnp.int32, (ROWS, COLS), 0)
    query_at = lax.broadcasted_iota(jnp.int32, (ROWS, COLS), 1) % ROWS
    diag = jnp.where(key_at <= query_at, diag, MASKED)
    prev = jnp.where(seen, dot(table[before, :, :HEAD], queries, NT), MASKED)
    return diag, prev


def window_kernel(where_ref, q0_ref, q1_ref, kv0_ref, kv1_ref, out_ref, stat_ref, table, qs):
    _, blocks, place = geometry(where_ref)
    for k, ref in enumerate((kv0_ref, kv1_ref)):
        for s in range(2):
            table[2 * k + s] = ref[s]
    for i, q_ref in enumerate((q0_ref, q1_ref)):
        block = blocks[i]
        stack_heads(qs, q_ref)
        at, before = place(block), place(jnp.maximum(block - 1, 0))
        diag, prev = window_scores(table, at, before, block >= 1, qs[...])
        top = jnp.maximum(
            jnp.max(diag, axis=0, keepdims=True), jnp.max(prev, axis=0, keepdims=True)
        )
        diag = jnp.exp2((diag - top) * SCALE_LOG2E)
        prev = jnp.exp2((prev - top) * SCALE_LOG2E)
        total = jnp.sum(diag, axis=0, keepdims=True) + jnp.sum(prev, axis=0, keepdims=True)
        inv = 1.0 / jnp.maximum(total, 1.0)
        out_ref[i] = dot(table[at, :, HEAD:].T, (diag * inv).astype(BF16), NN) + dot(
            table[before, :, HEAD:].T, (prev * inv).astype(BF16), NN
        )
        stat_ref[i, 0:1, :] = top
        stat_ref[i, 1:2, :] = inv


def chosen_kernel(
    where_ref,
    offset_ref,
    count_ref,
    q0_ref,
    q1_ref,
    ct0_ref,
    ct1_ref,
    gain_ref,
    window_ref,
    kv1_ref,
    kv2_ref,
    kv3_ref,
    kv4_ref,
    out_ref,
    low_ref,
    inner_ref,
    gq_ref,
    g1_ref,
    g2_ref,
    g3_ref,
    g4_ref,
    table,
    soft,
    acc,
    qs,
    gain_t,
    ot,
):
    half, blocks, place = geometry(where_ref)
    for k, ref in enumerate((kv1_ref, kv2_ref, kv3_ref, kv4_ref)):
        for s in range(2):
            table[2 * k + s] = ref[s]
    acc[...] = jnp.zeros_like(acc)
    gains = gain_ref[pl.ds(half, 1), :]
    for n in range(GROUP):
        row = gains[:, n * HEAD : (n + 1) * HEAD]
        gain_t[:, n * ROWS : (n + 1) * ROWS] = jnp.broadcast_to(row, (ROWS, HEAD)).T

    for i, (q_ref, ct_ref) in enumerate(((q0_ref, ct0_ref), (q1_ref, ct1_ref))):
        block = blocks[i]
        stack_heads(qs, q_ref)
        count = count_ref[block]

        def slot_of(j):
            source = block - offset_ref[block * SEL + j]
            return source >= 0, place(jnp.maximum(source, 0)) - 2

        def each_slot(step, start):
            def run(j, carry):
                seen, at = slot_of(j)
                return lax.cond(seen, lambda c: step(j, at, c), lambda c: c, carry)

            return lax.fori_loop(0, count, run, start)

        def scores(j, at, top):
            s = dot(table[at, :, :HEAD], qs[...], NT)
            soft[j] = s
            return jnp.maximum(top, jnp.max(s, axis=0, keepdims=True))

        top = each_slot(scores, jnp.full((1, COLS), MASKED, F32))

        def expo(j, at, total):
            e = jnp.exp2((soft[j] - top) * SCALE_LOG2E)
            soft[j] = e
            return total + jnp.sum(e, axis=0, keepdims=True)

        inv = 1.0 / jnp.maximum(each_slot(expo, jnp.zeros((1, COLS), F32)), 1.0)
        ot[...] = jnp.zeros_like(ot)

        def weigh(j, at, carry):
            p = soft[j] * inv
            soft[j] = p
            ot[...] += dot(table[at, :, HEAD:].T, p.astype(BF16), NN)
            return carry

        each_slot(weigh, 0)

        out_w = window_ref[i]
        out_c = ot[...]
        summed = out_w + out_c
        inverse = lax.rsqrt(jnp.mean(summed * summed, axis=0, keepdims=True) + EPS)
        normed = summed * inverse
        gain = gain_t[...]
        out_t = normed * gain
        ct_t = jnp.concatenate(
            [ct_ref[:, n * HEAD : (n + 1) * HEAD].astype(F32).T for n in range(GROUP)], axis=1
        )
        grad_normed = ct_t * gain
        inner = jnp.mean(grad_normed * normed, axis=0, keepdims=True)
        grad_low = (inverse * (grad_normed - normed * inner)).astype(BF16)
        wide = grad_low.astype(F32)
        inner_ref[i] = jnp.sum(wide * out_w, axis=0, keepdims=True)
        inner_c = jnp.sum(wide * out_c, axis=0, keepdims=True)
        low_ref[i] = grad_low
        for n in range(GROUP):
            out_ref[i, :, n * HEAD : (n + 1) * HEAD] = out_t[
                :, n * ROWS : (n + 1) * ROWS
            ].T.astype(BF16)
        gq_ref[i] = jnp.zeros((HEAD, COLS), F32)

        def back(j, at, carry):
            p = soft[j]
            low = low_ref[i]
            grad_w = dot(table[at, :, HEAD:], low, NN)
            grad_s = (SCALE * p * (grad_w - inner_c)).astype(BF16)
            acc[at, :, HEAD:] += dot(p.astype(BF16), low, NT)
            acc[at, :, :HEAD] += dot(grad_s, qs[...], NN)
            gq_ref[i] += dot(table[at, :, :HEAD].T, grad_s, NN)
            return carry

        each_slot(back, 0)

    g1_ref[...] = acc[0:2]
    for k, ref in enumerate((g2_ref, g3_ref, g4_ref)):
        ref[...] = acc[2 * k + 2 : 2 * k + 4].astype(BF16)


def window_back_kernel(
    where_ref,
    q0_ref,
    q1_ref,
    kv0_ref,
    kv1_ref,
    stat_ref,
    low_ref,
    inner_ref,
    gqc_ref,
    g1c_ref,
    gq_ref,
    own_ref,
    g1_ref,
    table,
    acc,
    qs,
):
    _, blocks, place = geometry(where_ref)
    for k, ref in enumerate((kv0_ref, kv1_ref)):
        for s in range(2):
            table[2 * k + s] = ref[s]
    acc[0:2] = jnp.zeros((2, ROWS, 2 * HEAD), F32)
    acc[2:4] = g1c_ref[...]
    for i, q_ref in enumerate((q0_ref, q1_ref)):
        block = blocks[i]
        stack_heads(qs, q_ref)
        at, before = place(block), place(jnp.maximum(block - 1, 0))
        top = stat_ref[i, 0:1, :]
        inv = stat_ref[i, 1:2, :]
        low = low_ref[i]
        inner = inner_ref[i]
        gqt = gqc_ref[i]
        both = window_scores(table, at, before, block >= 1, qs[...])
        for where, s in zip((at, before), both):
            p = jnp.exp2((s - top) * SCALE_LOG2E) * inv
            grad_w = dot(table[where, :, HEAD:], low, NN)
            grad_s = (SCALE * p * (grad_w - inner)).astype(BF16)
            acc[where, :, HEAD:] += dot(p.astype(BF16), low, NT)
            acc[where, :, :HEAD] += dot(grad_s, qs[...], NN)
            gqt = gqt + dot(table[where, :, :HEAD].T, grad_s, NN)
        for n in range(GROUP):
            gq_ref[i, :, n * HEAD : (n + 1) * HEAD] = gqt[:, n * ROWS : (n + 1) * ROWS].T.astype(
                BF16
            )
    own_ref[...] = acc[0:2]
    g1_ref[...] = acc[2:4].astype(BF16)


VMEM = pl.BlockSpec(memory_space=pltpu.VMEM)
SMEM = pl.BlockSpec(memory_space=pltpu.SMEM)
PAIR = (2, ROWS, 2 * HEAD)
WIDE = (2, HEAD, COLS)
NATURAL = (2, ROWS, HALF)


def table_of(blocks, dtype):
    return pltpu.VMEM((blocks, ROWS, 2 * HEAD), dtype)


def call(kernel, name, scalars, args, outs, scratch, flops, limit):
    return pl.pallas_call(
        kernel,
        out_shape=[jax.ShapeDtypeStruct(*out) for out in outs],
        in_specs=[SMEM] * scalars + [VMEM] * (len(args) - scalars),
        out_specs=[VMEM] * len(outs),
        scratch_shapes=scratch,
        compiler_params=pltpu.CompilerParams(vmem_limit_bytes=limit << 20),
        cost_estimate=pl.CostEstimate(flops=flops, bytes_accessed=4_000_000, transcendentals=0),
        name=name,
    )(*args)


def per_device(queries, key_rows, value_rows, chosen_offset, chosen_count, head_gain, cotangent):
    size = lax.axis_size(AXES)
    groups = lax.axis_size("grp")
    side = 4
    me = lax.axis_index(AXES)
    half = me % 2

    def move(x, target):
        return lax.ppermute(x, AXES, [(i, target(i)) for i in range(size)])

    def swap(x):
        return move(x, lambda i: i ^ 1)

    def on(k):
        return lambda i: (i + 2 * k) % size

    def relay(i):
        ctx, grp = divmod(i, groups)
        top, x, y = ctx // side**2, ctx // side % side, ctx % side
        top = top ^ int(x == side - 1 and y >= side - 2)
        return ((top * side + x) * side + (y - 1) % side) * groups + grp

    relayed = {relay(i): i for i in range(size)}

    def onward(i):
        return on(4)(relayed[i])

    def backward(target):
        from_ = {target(i): i for i in range(size)}
        return lambda i: from_[i]

    def part(x, which, width):
        return lax.dynamic_slice(x, (0, which * width), (x.shape[0], width))

    def head_of(which):
        return jnp.concatenate([part(key_rows, which, HEAD), part(value_rows, which, HEAD)], axis=1)

    other = 1 - half
    own = jnp.stack([head_of(half), swap(head_of(other))])
    kv2 = move(own, on(2))
    half4 = move(own, relay)
    kv1 = move(own, on(1))
    kv3 = move(kv2, on(1))
    kv4 = move(half4, onward)

    where = me.astype(jnp.int32).reshape(1)
    q0, q1 = part(queries, half, HALF), swap(part(queries, other, HALF))
    ct0, ct1 = part(cotangent, half, HALF), swap(part(cotangent, other, HALF))
    window, stats = call(
        window_kernel,
        "window",
        1,
        (where, q0, q1, own, kv1),
        ((WIDE, F32), ((2, 2, COLS), F32)),
        [table_of(4, BF16), pltpu.VMEM((COLS, HEAD), BF16)],
        800_000_000,
        32,
    )
    out, low, inner, gq_chosen, g1_chosen, g2, g3, g4 = call(
        chosen_kernel,
        "chosen",
        3,
        (
            where,
            chosen_offset.reshape(-1),
            chosen_count,
            q0,
            q1,
            ct0,
            ct1,
            head_gain.reshape(2, HALF),
            window,
            kv1,
            kv2,
            kv3,
            kv4,
        ),
        (
            (NATURAL, BF16),
            (WIDE, BF16),
            ((2, 1, COLS), F32),
            (WIDE, F32),
            (PAIR, F32),
            (PAIR, BF16),
            (PAIR, BF16),
            (PAIR, BF16),
        ),
        [
            table_of(8, BF16),
            pltpu.VMEM((SEL, ROWS, COLS), F32),
            table_of(8, F32),
            pltpu.VMEM((COLS, HEAD), BF16),
            pltpu.VMEM((HEAD, COLS), F32),
            pltpu.VMEM((HEAD, COLS), F32),
        ],
        3_000_000_000,
        40,
    )
    back3 = move(g3, backward(on(1)))
    half4 = move(g4, backward(onward))
    gq, grad_own, g1 = call(
        window_back_kernel,
        "window_back",
        1,
        (where, q0, q1, own, kv1, stats, low, inner, gq_chosen, g1_chosen),
        ((NATURAL, BF16), (PAIR, F32), (PAIR, BF16)),
        [table_of(4, BF16), table_of(4, F32), pltpu.VMEM((COLS, HEAD), BF16)],
        1_600_000_000,
        40,
    )
    back2 = move((g2.astype(F32) + back3.astype(F32)).astype(BF16), backward(on(2)))
    back4 = move(half4, backward(relay))
    back1 = move(g1, backward(on(1)))
    total = grad_own + back1.astype(F32) + back2.astype(F32) + back4.astype(F32)
    total = total.astype(BF16)

    def joined(mine, theirs):
        return jnp.where(
            half == 0,
            jnp.concatenate([mine, theirs], axis=1),
            jnp.concatenate([theirs, mine], axis=1),
        )

    theirs = swap(total[1])
    return (
        joined(out[0], swap(out[1])),
        joined(gq[0], swap(gq[1])),
        joined(total[0, :, :HEAD], theirs[:, :HEAD]),
        joined(total[0, :, HEAD:], theirs[:, HEAD:]),
    )


def solution(mesh):
    rows = P(AXES, None)
    return jax.shard_map(
        per_device,
        mesh=mesh,
        in_specs=(rows, rows, rows, P(), P(), P(), rows),
        out_specs=(rows, rows, rows, rows),
        check_vma=False,
    )
```

```python
import math

import jax
import jax.numpy as jnp
from jax import lax
from jax.experimental import pallas as pl
from jax.experimental.pallas import tpu as pltpu
from jax.sharding import PartitionSpec as P


AXES = ("ctx", "grp")
ROWS = 256
HEAD = 128
GROUP = 4
HALF = GROUP * HEAD
COLS = GROUP * ROWS
SEL = 4
BLOCKS = 128
SCALE = HEAD**-0.5
SCALE_LOG2E = SCALE * math.log2(math.e)
MASKED = -1e30
FLOOR = -1e29
EPS = 1e-06

NT = (((1,), (1,)), ((), ()))
NN = (((1,), (0,)), ((), ()))
F32 = jnp.float32
BF16 = jnp.bfloat16


def dot(a, b, dims):
    return lax.dot_general(a, b, dims, preferred_element_type=F32)


def geometry(where_ref):
    me = where_ref[0]
    half = me % 2
    chip = me // 2

    def place(block):
        return 2 * (chip - block // 2) + (block % 2 + half) % 2

    return half, (me, me + 1 - 2 * half), place


def stack_heads(qs, q_ref):
    for n in range(GROUP):
        qs[n * ROWS : (n + 1) * ROWS, :] = q_ref[:, n * HEAD : (n + 1) * HEAD]


def window_scores(table, at, before, seen, queries):
    diag = dot(table[at, :, :HEAD], queries, NT)
    key_at = lax.broadcasted_iota(jnp.int32, (ROWS, COLS), 0)
    query_at = lax.broadcasted_iota(jnp.int32, (ROWS, COLS), 1) % ROWS
    diag = jnp.where(key_at <= query_at, diag, MASKED)
    prev = jnp.where(seen, dot(table[before, :, :HEAD], queries, NT), MASKED)
    return diag, prev


def load_table(table, *refs):
    for k, ref in enumerate(refs):
        for s in range(2):
            table[2 * k + s] = ref[s]


def window_kernel(
    where_ref,
    q0_ref,
    q1_ref,
    ct0_ref,
    ct1_ref,
    gain_ref,
    kv0_ref,
    kv1_ref,
    out_ref,
    stat_ref,
    gain_t_ref,
    normed_ref,
    table,
    qs,
):
    half, blocks, place = geometry(where_ref)
    load_table(table, kv0_ref, kv1_ref)
    gains = gain_ref[pl.ds(half, 1), :]
    for n in range(GROUP):
        row = gains[:, n * HEAD : (n + 1) * HEAD]
        gain_t_ref[:, n * ROWS : (n + 1) * ROWS] = jnp.broadcast_to(row, (ROWS, HEAD)).T
    for i, (q_ref, ct_ref) in enumerate(((q0_ref, ct0_ref), (q1_ref, ct1_ref))):
        block = blocks[i]
        stack_heads(qs, q_ref)
        for n in range(GROUP):
            at = slice(n * ROWS, (n + 1) * ROWS)
            ct_t = ct_ref[:, n * HEAD : (n + 1) * HEAD].astype(F32).T
            normed_ref[i, :, at] = ct_t * gain_t_ref[:, at]
        at, before = place(block), place(jnp.maximum(block - 1, 0))
        diag, prev = window_scores(table, at, before, block >= 1, qs[...])
        top = jnp.maximum(
            jnp.max(diag, axis=0, keepdims=True), jnp.max(prev, axis=0, keepdims=True)
        )
        diag = jnp.exp2((diag - top) * SCALE_LOG2E)
        prev = jnp.exp2((prev - top) * SCALE_LOG2E)
        total = jnp.sum(diag, axis=0, keepdims=True) + jnp.sum(prev, axis=0, keepdims=True)
        inv = 1.0 / jnp.maximum(total, 1.0)
        out_ref[i] = dot(table[at, :, HEAD:].T, (diag * inv).astype(BF16), NN) + dot(
            table[before, :, HEAD:].T, (prev * inv).astype(BF16), NN
        )
        stat_ref[i, 0:1, :] = top
        stat_ref[i, 1:2, :] = inv


def slots_of(block, offset_ref, place):
    count = offset_ref[BLOCKS * SEL + block]
    seen, places = [], []
    for j in range(SEL):
        source = block - offset_ref[block * SEL + j]
        seen.append((source >= 0) & (j < count))
        places.append(place(jnp.maximum(source, 0)))
    return count, seen, places


def ranked(flags, values):
    number = jnp.int32(0)
    order = [jnp.int32(0)] * SEL
    for flag, value in zip(flags, values):
        for r in range(SEL):
            order[r] = jnp.where(flag & (number == r), value, order[r])
        number = number + flag.astype(jnp.int32)
    return number, order


def back_step(table, acc, at, to, p, queries, low, inner):
    grad_w = dot(table[at, :, HEAD:], low, NN)
    grad_s = (SCALE * p * (grad_w - inner)).astype(BF16)
    acc[to, :, HEAD:] += dot(p.astype(BF16), low, NT)
    acc[to, :, :HEAD] += dot(grad_s, queries, NN)
    return dot(table[at, :, :HEAD].T, grad_s, NN)


def chosen_kernel(
    where_ref,
    offset_ref,
    q0_ref,
    q1_ref,
    gain_t_ref,
    normed_ref,
    window_ref,
    kv1_ref,
    kv2_ref,
    kv3_ref,
    kv4_ref,
    out_ref,
    low_ref,
    inner_ref,
    stat_ref,
    gq_ref,
    g3_ref,
    g4_ref,
    table,
    soft,
    acc,
    qs,
    ot,
):
    half, _, place = geometry(where_ref)
    me = where_ref[0]
    load_table(table, kv1_ref, kv2_ref, kv3_ref, kv4_ref)
    acc[...] = jnp.zeros_like(acc)
    stack_heads(qs.at[0], q0_ref)
    stack_heads(qs.at[1], q1_ref)

    def one_block(i, carry):
        block = me + i * (1 - 2 * half)
        count, seen, places = slots_of(block, offset_ref, place)

        def forward(slots):
            queries = qs[i]
            scores = []
            top = jnp.full((1, COLS), FLOOR, F32)
            spots = [jnp.where(ok, at - 2, 0) for ok, at in zip(seen, places)]
            for j in range(slots):
                s = jnp.where(seen[j], dot(table[spots[j], :, :HEAD], queries, NT), MASKED)
                top = jnp.maximum(top, jnp.max(s, axis=0, keepdims=True))
                scores.append(s)
            total = jnp.zeros((1, COLS), F32)
            for j in range(slots):
                scores[j] = jnp.exp2((scores[j] - top) * SCALE_LOG2E)
                total = total + jnp.sum(scores[j], axis=0, keepdims=True)
            inv = 1.0 / jnp.maximum(total, 1.0)
            out = jnp.zeros((HEAD, COLS), F32)
            for j in range(slots):
                p = scores[j] * inv
                soft[j] = p
                out = out + dot(table[spots[j], :, HEAD:].T, p.astype(BF16), NN)
            ot[...] = out
            stat_ref[i, 0:1, :] = top
            stat_ref[i, 1:2, :] = inv

        for slots in range(SEL + 1):
            pl.when(count == slots)(lambda slots=slots: forward(slots))

        out_w = window_ref[i]
        out_c = ot[...]
        summed = out_w + out_c
        inverse = lax.rsqrt(jnp.mean(summed * summed, axis=0, keepdims=True) + EPS)
        normed = summed * inverse
        out_t = normed * gain_t_ref[...]
        grad_normed = normed_ref[i]
        inner = jnp.mean(grad_normed * normed, axis=0, keepdims=True)
        low = (inverse * (grad_normed - normed * inner)).astype(BF16)
        wide = low.astype(F32)
        inner_c = jnp.sum(wide * out_c, axis=0, keepdims=True)
        inner_ref[i, 0:1, :] = jnp.sum(wide * out_w, axis=0, keepdims=True)
        inner_ref[i, 1:2, :] = inner_c
        low_ref[i] = low
        for n in range(GROUP):
            out_ref[i, :, n * HEAD : (n + 1) * HEAD] = out_t[
                :, n * ROWS : (n + 1) * ROWS
            ].T.astype(BF16)

        far = [s & (p >= 6) for s, p in zip(seen, places)]
        number, slot = ranked(far, range(SEL))
        _, spot = ranked(far, places)

        def backward(slots):
            gq = jnp.zeros((HEAD, COLS), F32)
            for r in range(slots):
                at = spot[r] - 2
                gq = gq + back_step(
                    table, acc, at, spot[r] - 6, soft[slot[r]], qs[i], low_ref[i], inner_c
                )
            gq_ref[i] = gq

        for slots in range(SEL + 1):
            pl.when(number == slots)(lambda slots=slots: backward(slots))
        return carry

    lax.fori_loop(0, 2, one_block, 0)
    g3_ref[...] = acc[0:2].astype(BF16)
    g4_ref[...] = acc[2:4].astype(BF16)


def near_kernel(
    where_ref,
    offset_ref,
    q0_ref,
    q1_ref,
    kv0_ref,
    kv1_ref,
    kv2_ref,
    statw_ref,
    statc_ref,
    low_ref,
    inner_ref,
    gqc_ref,
    gq_ref,
    own_ref,
    g1_ref,
    g2_ref,
    table,
    acc,
    qs,
    gqt,
):
    half, _, place = geometry(where_ref)
    me = where_ref[0]
    load_table(table, kv0_ref, kv1_ref, kv2_ref)
    acc[...] = jnp.zeros_like(acc)
    stack_heads(qs.at[0], q0_ref)
    stack_heads(qs.at[1], q1_ref)

    def one_block(i, carry):
        block = me + i * (1 - 2 * half)
        at, before = place(block), place(jnp.maximum(block - 1, 0))
        queries = qs[i]
        low = low_ref[i]
        top = statw_ref[i, 0:1, :]
        inv = statw_ref[i, 1:2, :]
        inner = inner_ref[i, 0:1, :]
        gq = gqc_ref[i]
        both = window_scores(table, at, before, block >= 1, queries)
        for spot, s in zip((at, before), both):
            p = jnp.exp2((s - top) * SCALE_LOG2E) * inv
            gq = gq + back_step(table, acc, spot, spot, p, queries, low, inner)
        gqt[...] = gq

        _, seen, places = slots_of(block, offset_ref, place)
        number, spots = ranked([s & (p < 6) for s, p in zip(seen, places)], places)

        def chosen(slots):
            queries = qs[i]
            low = low_ref[i]
            top = statc_ref[i, 0:1, :]
            inv = statc_ref[i, 1:2, :]
            inner = inner_ref[i, 1:2, :]
            gq = gqt[...]
            for r in range(slots):
                s = dot(table[spots[r], :, :HEAD], queries, NT)
                p = jnp.exp2((s - top) * SCALE_LOG2E) * inv
                gq = gq + back_step(table, acc, spots[r], spots[r], p, queries, low, inner)
            for n in range(GROUP):
                gq_ref[i, :, n * HEAD : (n + 1) * HEAD] = gq[
                    :, n * ROWS : (n + 1) * ROWS
                ].T.astype(BF16)

        for slots in range(SEL + 1):
            pl.when(number == slots)(lambda slots=slots: chosen(slots))
        return carry

    lax.fori_loop(0, 2, one_block, 0)
    own_ref[...] = acc[0:2]
    g1_ref[...] = acc[2:4].astype(BF16)
    g2_ref[...] = acc[4:6].astype(BF16)


def finish_kernel(own_ref, a_ref, b_ref, c_ref, mine_ref, theirs_ref):
    for s, ref in enumerate((mine_ref, theirs_ref)):
        total = own_ref[s] + a_ref[s].astype(F32) + b_ref[s].astype(F32) + c_ref[s].astype(F32)
        ref[...] = total.astype(BF16)


def join_kernel(where_ref, mine_ref, theirs_ref, gk_ref, gv_ref):
    first = where_ref[0] % 2 == 0
    for n, ref in enumerate((gk_ref, gv_ref)):
        at = slice(n * HEAD, (n + 1) * HEAD)
        mine, theirs = mine_ref[:, at], theirs_ref[:, at]
        ref[:, :HEAD] = jnp.where(first, mine, theirs)
        ref[:, HEAD:] = jnp.where(first, theirs, mine)


VMEM = pl.BlockSpec(memory_space=pltpu.VMEM)
SMEM = pl.BlockSpec(memory_space=pltpu.SMEM)
PAIR = (2, ROWS, 2 * HEAD)
WIDE = (2, HEAD, COLS)
NATURAL = (2, ROWS, HALF)


def table_of(blocks, dtype):
    return pltpu.VMEM((blocks, ROWS, 2 * HEAD), dtype)


def call(kernel, scalars, args, outs, scratch, flops, limit):
    return pl.pallas_call(
        kernel,
        out_shape=[jax.ShapeDtypeStruct(*out) for out in outs],
        in_specs=[SMEM] * scalars + [VMEM] * (len(args) - scalars),
        out_specs=[VMEM] * len(outs),
        scratch_shapes=scratch,
        compiler_params=pltpu.CompilerParams(vmem_limit_bytes=limit << 20),
        cost_estimate=pl.CostEstimate(flops=flops, bytes_accessed=4_000_000, transcendentals=0),
    )(*args)


def per_device(queries, key_rows, value_rows, chosen_offset, chosen_count, head_gain, cotangent):
    size = lax.axis_size(AXES)
    groups = lax.axis_size("grp")
    side = 4
    me = lax.axis_index(AXES)
    half = me % 2

    def move(x, target):
        return lax.ppermute(x, AXES, [(i, target(i)) for i in range(size)])

    def swap(x):
        return move(x, lambda i: i ^ 1)

    def on(k):
        return lambda i: (i + 2 * k) % size

    def relay(i):
        ctx, grp = divmod(i, groups)
        top, x, y = ctx // side**2, ctx // side % side, ctx % side
        top = top ^ int(x == side - 1 and y >= side - 2)
        return ((top * side + x) * side + (y - 1) % side) * groups + grp

    relayed = {relay(i): i for i in range(size)}

    def onward(i):
        return on(4)(relayed[i])

    def backward(target):
        from_ = {target(i): i for i in range(size)}
        return lambda i: from_[i]

    def part(x, which, width):
        return lax.dynamic_slice(x, (0, which * width), (x.shape[0], width))

    def head_of(which):
        return jnp.concatenate([part(key_rows, which, HEAD), part(value_rows, which, HEAD)], axis=1)

    other = 1 - half
    own = jnp.stack([head_of(half), swap(head_of(other))])
    kv2 = move(own, on(2))
    half4 = move(own, relay)
    kv1 = move(own, on(1))
    kv3 = move(kv2, on(1))
    kv4 = move(half4, onward)

    where = me.astype(jnp.int32).reshape(1)
    q0, q1 = part(queries, half, HALF), swap(part(queries, other, HALF))
    ct0, ct1 = part(cotangent, half, HALF), swap(part(cotangent, other, HALF))
    stat = ((2, 2, COLS), F32)
    offsets = jnp.concatenate([chosen_offset.reshape(-1), chosen_count])
    queues = pltpu.VMEM((2, COLS, HEAD), BF16)
    window, window_stats, gain_t, normed = call(
        window_kernel,
        1,
        (where, q0, q1, ct0, ct1, head_gain.reshape(2, HALF), own, kv1),
        ((WIDE, F32), stat, ((HEAD, COLS), F32), (WIDE, F32)),
        [table_of(4, BF16), pltpu.VMEM((COLS, HEAD), BF16)],
        800_000_000,
        32,
    )
    out, low, inner, chosen_stats, gq_far, g3, g4 = call(
        chosen_kernel,
        2,
        (where, offsets, q0, q1, gain_t, normed, window, kv1, kv2, kv3, kv4),
        ((NATURAL, BF16), (WIDE, BF16), stat, stat, (WIDE, F32), (PAIR, BF16), (PAIR, BF16)),
        [
            table_of(8, BF16),
            pltpu.VMEM((SEL, ROWS, COLS), F32),
            table_of(4, F32),
            queues,
            pltpu.VMEM((HEAD, COLS), F32),
        ],
        2_500_000_000,
        40,
    )
    back3 = move(g3, backward(on(1)))
    half4 = move(g4, backward(onward))
    gq, grad_own, g1, g2 = call(
        near_kernel,
        2,
        (
            where,
            offsets,
            q0,
            q1,
            own,
            kv1,
            kv2,
            window_stats,
            chosen_stats,
            low,
            inner,
            gq_far,
        ),
        ((NATURAL, BF16), (PAIR, F32), (PAIR, BF16), (PAIR, BF16)),
        [table_of(6, BF16), table_of(6, F32), queues, pltpu.VMEM((HEAD, COLS), F32)],
        2_500_000_000,
        40,
    )
    back2 = move((g2.astype(F32) + back3.astype(F32)).astype(BF16), backward(on(2)))
    back4 = move(half4, backward(relay))
    back1 = move(g1, backward(on(1)))
    square = ((ROWS, 2 * HEAD), BF16)
    mine, send = call(
        finish_kernel, 0, (grad_own, back1, back2, back4), (square, square), [], 0, 16
    )
    theirs = swap(send)
    gk, gv = call(join_kernel, 1, (where, mine, theirs), (square, square), [], 0, 16)

    def joined(mine, theirs):
        return jnp.where(
            half == 0,
            jnp.concatenate([mine, theirs], axis=1),
            jnp.concatenate([theirs, mine], axis=1),
        )

    out_other, gq_other = swap(out[1]), swap(gq[1])
    out = joined(out[0], out_other)
    gq = joined(gq[0], gq_other)
    return (
        out,
        gq,
        gk,
        gv,
    )


def solution(mesh):
    rows = P(AXES, None)
    return jax.shard_map(
        per_device,
        mesh=mesh,
        in_specs=(rows, rows, rows, P(), P(), P(), rows),
        out_specs=(rows, rows, rows, rows),
        check_vma=False,
    )
```

```python
import math

import jax
import jax.numpy as jnp
from jax import lax
from jax.experimental import pallas as pl
from jax.experimental.pallas import tpu as pltpu
from jax.sharding import PartitionSpec as P


AXES = ("ctx", "grp")
ROWS = 256
HEAD = 128
GROUP = 4
HALF = GROUP * HEAD
COLS = GROUP * ROWS
SEL = 4
BLOCKS = 128
SCALE = HEAD**-0.5
SCALE_LOG2E = SCALE * math.log2(math.e)
MASKED = -1e30
FLOOR = -1e29
EPS = 1e-06

NT = (((1,), (1,)), ((), ()))
NN = (((1,), (0,)), ((), ()))
F32 = jnp.float32
BF16 = jnp.bfloat16


def dot(a, b, dims):
    return lax.dot_general(a, b, dims, preferred_element_type=F32)


def geometry(where_ref):
    me = where_ref[0]
    half = me % 2
    chip = me // 2

    def place(block):
        return 2 * (chip - block // 2) + (block % 2 + half) % 2

    return half, (me, me + 1 - 2 * half), place


def stack_heads(qs, q_ref):
    for n in range(GROUP):
        qs[n * ROWS : (n + 1) * ROWS, :] = q_ref[:, n * HEAD : (n + 1) * HEAD]


def window_scores(table, at, before, seen, queries):
    diag = dot(table[at, :, :HEAD], queries, NT)
    key_at = lax.broadcasted_iota(jnp.int32, (ROWS, COLS), 0)
    query_at = lax.broadcasted_iota(jnp.int32, (ROWS, COLS), 1) % ROWS
    diag = jnp.where(key_at <= query_at, diag, MASKED)
    prev = jnp.where(seen, dot(table[before, :, :HEAD], queries, NT), MASKED)
    return diag, prev


def load_table(table, *refs):
    for k, ref in enumerate(refs):
        for s in range(2):
            table[2 * k + s] = ref[s]


def slots_of(block, offset_ref, place):
    count = offset_ref[BLOCKS * SEL + block]
    seen, places = [], []
    for j in range(SEL):
        source = block - offset_ref[block * SEL + j]
        seen.append((source >= 0) & (j < count))
        places.append(place(jnp.maximum(source, 0)))
    return count, seen, places


def ranked(flags, values):
    number = jnp.int32(0)
    order = [jnp.int32(0)] * SEL
    for flag, value in zip(flags, values):
        for r in range(SEL):
            order[r] = jnp.where(flag & (number == r), value, order[r])
        number = number + flag.astype(jnp.int32)
    return number, order


def window_kernel(
    where_ref,
    offset_ref,
    q0_ref,
    q1_ref,
    ct0_ref,
    ct1_ref,
    gain_ref,
    kv0_ref,
    kv1_ref,
    kv2_ref,
    out_ref,
    stat_ref,
    gain_t_ref,
    normed_ref,
    near_ref,
    near_stat_ref,
    table,
    qs,
):
    half, _, place = geometry(where_ref)
    me = where_ref[0]
    load_table(table, kv0_ref, kv1_ref, kv2_ref)
    gains = gain_ref[pl.ds(half, 1), :]
    for n in range(GROUP):
        row = gains[:, n * HEAD : (n + 1) * HEAD]
        gain_t_ref[:, n * ROWS : (n + 1) * ROWS] = jnp.broadcast_to(row, (ROWS, HEAD)).T
    for i, (q_ref, ct_ref) in enumerate(((q0_ref, ct0_ref), (q1_ref, ct1_ref))):
        stack_heads(qs.at[i], q_ref)
        for n in range(GROUP):
            at = slice(n * ROWS, (n + 1) * ROWS)
            ct_t = ct_ref[:, n * HEAD : (n + 1) * HEAD].astype(F32).T
            normed_ref[i, :, at] = ct_t * gain_t_ref[:, at]

    def one_block(i, carry):
        block = me + i * (1 - 2 * half)
        at, before = place(block), place(jnp.maximum(block - 1, 0))
        diag, prev = window_scores(table, at, before, block >= 1, qs[i])
        top = jnp.maximum(
            jnp.max(diag, axis=0, keepdims=True), jnp.max(prev, axis=0, keepdims=True)
        )
        diag = jnp.exp2((diag - top) * SCALE_LOG2E)
        prev = jnp.exp2((prev - top) * SCALE_LOG2E)
        total = jnp.sum(diag, axis=0, keepdims=True) + jnp.sum(prev, axis=0, keepdims=True)
        inv = 1.0 / jnp.maximum(total, 1.0)
        out_ref[i] = dot(table[at, :, HEAD:].T, (diag * inv).astype(BF16), NN) + dot(
            table[before, :, HEAD:].T, (prev * inv).astype(BF16), NN
        )
        stat_ref[i, 0:1, :] = top
        stat_ref[i, 1:2, :] = inv

        _, seen, places = slots_of(block, offset_ref, place)
        number, spots = ranked([s & (p < 6) for s, p in zip(seen, places)], places)

        def near(slots):
            queries = qs[i]
            scores = [dot(table[spots[r], :, :HEAD], queries, NT) for r in range(slots)]
            top = jnp.full((1, COLS), FLOOR, F32)
            for s in scores:
                top = jnp.maximum(top, jnp.max(s, axis=0, keepdims=True))
            total = jnp.zeros((1, COLS), F32)
            out = jnp.zeros((HEAD, COLS), F32)
            for r, s in enumerate(scores):
                e = jnp.exp2((s - top) * SCALE_LOG2E)
                total = total + jnp.sum(e, axis=0, keepdims=True)
                out = out + dot(table[spots[r], :, HEAD:].T, e.astype(BF16), NN)
            near_ref[i] = out
            near_stat_ref[i, 0:1, :] = top
            near_stat_ref[i, 1:2, :] = total

        for slots in range(SEL + 1):
            pl.when(number == slots)(lambda slots=slots: near(slots))
        return carry

    lax.fori_loop(0, 2, one_block, 0)


def back_step(table, acc, at, to, p, queries, low, inner):
    grad_w = dot(table[at, :, HEAD:], low, NN)
    grad_s = (SCALE * p * (grad_w - inner)).astype(BF16)
    acc[to, :, HEAD:] += dot(p.astype(BF16), low, NT)
    acc[to, :, :HEAD] += dot(grad_s, queries, NN)
    return dot(table[at, :, :HEAD].T, grad_s, NN)


def chosen_kernel(
    where_ref,
    offset_ref,
    q0_ref,
    q1_ref,
    gain_t_ref,
    normed_ref,
    window_ref,
    near_ref,
    near_stat_ref,
    kv3_ref,
    kv4_ref,
    out_ref,
    low_ref,
    inner_ref,
    stat_ref,
    gq_ref,
    g3_ref,
    g4_ref,
    table,
    soft,
    acc,
    qs,
    ot,
):
    half, _, place = geometry(where_ref)
    me = where_ref[0]
    load_table(table, kv3_ref, kv4_ref)
    acc[...] = jnp.zeros_like(acc)
    stack_heads(qs.at[0], q0_ref)
    stack_heads(qs.at[1], q1_ref)

    def one_block(i, carry):
        block = me + i * (1 - 2 * half)
        _, seen, places = slots_of(block, offset_ref, place)
        number, spots = ranked([s & (p >= 6) for s, p in zip(seen, places)], places)

        def forward(slots):
            queries = qs[i]
            near_top = near_stat_ref[i, 0:1, :]
            top = near_top
            scores = []
            for r in range(slots):
                s = dot(table[spots[r] - 6, :, :HEAD], queries, NT)
                top = jnp.maximum(top, jnp.max(s, axis=0, keepdims=True))
                scores.append(s)
            alpha = jnp.exp2((near_top - top) * SCALE_LOG2E)
            total = near_stat_ref[i, 1:2, :] * alpha
            for r in range(slots):
                scores[r] = jnp.exp2((scores[r] - top) * SCALE_LOG2E)
                total = total + jnp.sum(scores[r], axis=0, keepdims=True)
            inv = 1.0 / jnp.maximum(total, 1.0)
            out = near_ref[i] * (alpha * inv)
            for r in range(slots):
                p = scores[r] * inv
                soft[r] = p
                out = out + dot(table[spots[r] - 6, :, HEAD:].T, p.astype(BF16), NN)
            ot[...] = out
            stat_ref[i, 0:1, :] = top
            stat_ref[i, 1:2, :] = inv

        for slots in range(SEL + 1):
            pl.when(number == slots)(lambda slots=slots: forward(slots))

        out_w = window_ref[i]
        out_c = ot[...]
        summed = out_w + out_c
        inverse = lax.rsqrt(jnp.mean(summed * summed, axis=0, keepdims=True) + EPS)
        normed = summed * inverse
        out_t = normed * gain_t_ref[...]
        grad_normed = normed_ref[i]
        inner = jnp.mean(grad_normed * normed, axis=0, keepdims=True)
        low = (inverse * (grad_normed - normed * inner)).astype(BF16)
        wide = low.astype(F32)
        inner_c = jnp.sum(wide * out_c, axis=0, keepdims=True)
        inner_ref[i, 0:1, :] = jnp.sum(wide * out_w, axis=0, keepdims=True)
        inner_ref[i, 1:2, :] = inner_c
        low_ref[i] = low
        for n in range(GROUP):
            out_ref[i, :, n * HEAD : (n + 1) * HEAD] = out_t[
                :, n * ROWS : (n + 1) * ROWS
            ].T.astype(BF16)

        def backward(slots):
            gq = jnp.zeros((HEAD, COLS), F32)
            for r in range(slots):
                at = spots[r] - 6
                gq = gq + back_step(table, acc, at, at, soft[r], qs[i], low_ref[i], inner_c)
            gq_ref[i] = gq

        for slots in range(SEL + 1):
            pl.when(number == slots)(lambda slots=slots: backward(slots))
        return carry

    lax.fori_loop(0, 2, one_block, 0)
    g3_ref[...] = acc[0:2].astype(BF16)
    g4_ref[...] = acc[2:4].astype(BF16)


def near_kernel(
    where_ref,
    offset_ref,
    q0_ref,
    q1_ref,
    kv0_ref,
    kv1_ref,
    kv2_ref,
    statw_ref,
    statc_ref,
    low_ref,
    inner_ref,
    gqc_ref,
    gq_ref,
    own_ref,
    g1_ref,
    g2_ref,
    table,
    acc,
    qs,
    gqt,
):
    half, _, place = geometry(where_ref)
    me = where_ref[0]
    load_table(table, kv0_ref, kv1_ref, kv2_ref)
    acc[...] = jnp.zeros_like(acc)
    stack_heads(qs.at[0], q0_ref)
    stack_heads(qs.at[1], q1_ref)

    def one_block(i, carry):
        block = me + i * (1 - 2 * half)
        at, before = place(block), place(jnp.maximum(block - 1, 0))
        queries = qs[i]
        low = low_ref[i]
        top = statw_ref[i, 0:1, :]
        inv = statw_ref[i, 1:2, :]
        inner = inner_ref[i, 0:1, :]
        gq = gqc_ref[i]
        both = window_scores(table, at, before, block >= 1, queries)
        for spot, s in zip((at, before), both):
            p = jnp.exp2((s - top) * SCALE_LOG2E) * inv
            gq = gq + back_step(table, acc, spot, spot, p, queries, low, inner)
        gqt[...] = gq

        _, seen, places = slots_of(block, offset_ref, place)
        number, spots = ranked([s & (p < 6) for s, p in zip(seen, places)], places)

        def chosen(slots):
            queries = qs[i]
            low = low_ref[i]
            top = statc_ref[i, 0:1, :]
            inv = statc_ref[i, 1:2, :]
            inner = inner_ref[i, 1:2, :]
            gq = gqt[...]
            for r in range(slots):
                s = dot(table[spots[r], :, :HEAD], queries, NT)
                p = jnp.exp2((s - top) * SCALE_LOG2E) * inv
                gq = gq + back_step(table, acc, spots[r], spots[r], p, queries, low, inner)
            for n in range(GROUP):
                gq_ref[i, :, n * HEAD : (n + 1) * HEAD] = gq[
                    :, n * ROWS : (n + 1) * ROWS
                ].T.astype(BF16)

        for slots in range(SEL + 1):
            pl.when(number == slots)(lambda slots=slots: chosen(slots))
        return carry

    lax.fori_loop(0, 2, one_block, 0)
    own_ref[...] = acc[0:2]
    g1_ref[...] = acc[2:4].astype(BF16)
    g2_ref[...] = acc[4:6].astype(BF16)


def finish_kernel(own_ref, a_ref, b_ref, c_ref, mine_ref, theirs_ref):
    for s, ref in enumerate((mine_ref, theirs_ref)):
        total = own_ref[s] + a_ref[s].astype(F32) + b_ref[s].astype(F32) + c_ref[s].astype(F32)
        ref[...] = total.astype(BF16)


def join_kernel(where_ref, mine_ref, theirs_ref, gk_ref, gv_ref):
    first = where_ref[0] % 2 == 0
    for n, ref in enumerate((gk_ref, gv_ref)):
        at = slice(n * HEAD, (n + 1) * HEAD)
        mine, theirs = mine_ref[:, at], theirs_ref[:, at]
        ref[:, :HEAD] = jnp.where(first, mine, theirs)
        ref[:, HEAD:] = jnp.where(first, theirs, mine)


VMEM = pl.BlockSpec(memory_space=pltpu.VMEM)
SMEM = pl.BlockSpec(memory_space=pltpu.SMEM)
PAIR = (2, ROWS, 2 * HEAD)
WIDE = (2, HEAD, COLS)
NATURAL = (2, ROWS, HALF)


def table_of(blocks, dtype):
    return pltpu.VMEM((blocks, ROWS, 2 * HEAD), dtype)


def call(kernel, scalars, args, outs, scratch, flops, limit):
    return pl.pallas_call(
        kernel,
        out_shape=[jax.ShapeDtypeStruct(*out) for out in outs],
        in_specs=[SMEM] * scalars + [VMEM] * (len(args) - scalars),
        out_specs=[VMEM] * len(outs),
        scratch_shapes=scratch,
        compiler_params=pltpu.CompilerParams(vmem_limit_bytes=limit << 20),
        cost_estimate=pl.CostEstimate(flops=flops, bytes_accessed=4_000_000, transcendentals=0),
    )(*args)


def per_device(queries, key_rows, value_rows, chosen_offset, chosen_count, head_gain, cotangent):
    size = lax.axis_size(AXES)
    groups = lax.axis_size("grp")
    side = 4
    me = lax.axis_index(AXES)
    half = me % 2

    def move(x, target):
        return lax.ppermute(x, AXES, [(i, target(i)) for i in range(size)])

    def swap(x):
        return move(x, lambda i: i ^ 1)

    def on(k):
        return lambda i: (i + 2 * k) % size

    def relay(i):
        ctx, grp = divmod(i, groups)
        top, x, y = ctx // side**2, ctx // side % side, ctx % side
        top = top ^ int(x == side - 1 and y >= side - 2)
        return ((top * side + x) * side + (y - 1) % side) * groups + grp

    def relay_back(i):
        ctx, grp = divmod(i, groups)
        top, x, y = ctx // side**2, ctx // side % side, ctx % side
        top = top ^ int(x == 0 and y < 2)
        return ((top * side + x) * side + (y + 1) % side) * groups + grp

    relayed = {relay(i): i for i in range(size)}
    returned = {relay_back(i): i for i in range(size)}

    def onward(i):
        return on(4)(relayed[i])

    def backward(target):
        from_ = {target(i): i for i in range(size)}
        return lambda i: from_[i]

    def part(x, which, width):
        return lax.dynamic_slice(x, (0, which * width), (x.shape[0], width))

    def head_of(which):
        return jnp.concatenate([part(key_rows, which, HEAD), part(value_rows, which, HEAD)], axis=1)

    other = 1 - half
    own = jnp.stack([head_of(half), swap(head_of(other))])
    kv2 = move(own, on(2))
    half4 = move(own, relay)
    kv1 = move(own, on(1))
    kv3 = move(kv2, on(1))
    kv4 = move(half4, onward)

    where = me.astype(jnp.int32).reshape(1)
    q0, q1 = part(queries, half, HALF), swap(part(queries, other, HALF))
    ct0, ct1 = part(cotangent, half, HALF), swap(part(cotangent, other, HALF))
    stat = ((2, 2, COLS), F32)
    offsets = jnp.concatenate([chosen_offset.reshape(-1), chosen_count])
    queues = pltpu.VMEM((2, COLS, HEAD), BF16)
    window, window_stats, gain_t, normed, near, near_stats = call(
        window_kernel,
        2,
        (where, offsets, q0, q1, ct0, ct1, head_gain.reshape(2, HALF), own, kv1, kv2),
        ((WIDE, F32), stat, ((HEAD, COLS), F32), (WIDE, F32), (WIDE, F32), stat),
        [table_of(6, BF16), queues],
        800_000_000,
        32,
    )
    out, low, inner, chosen_stats, gq_far, g3, g4 = call(
        chosen_kernel,
        2,
        (where, offsets, q0, q1, gain_t, normed, window, near, near_stats, kv3, kv4),
        ((NATURAL, BF16), (WIDE, BF16), stat, stat, (WIDE, F32), (PAIR, BF16), (PAIR, BF16)),
        [
            table_of(4, BF16),
            pltpu.VMEM((SEL, ROWS, COLS), F32),
            table_of(4, F32),
            queues,
            pltpu.VMEM((HEAD, COLS), F32),
        ],
        2_500_000_000,
        40,
    )
    back3 = move(g3, backward(on(1)))
    half4 = move(g4, relay_back)
    gq, grad_own, g1, g2 = call(
        near_kernel,
        2,
        (
            where,
            offsets,
            q0,
            q1,
            own,
            kv1,
            kv2,
            window_stats,
            chosen_stats,
            low,
            inner,
            gq_far,
        ),
        ((NATURAL, BF16), (PAIR, F32), (PAIR, BF16), (PAIR, BF16)),
        [table_of(6, BF16), table_of(6, F32), queues, pltpu.VMEM((HEAD, COLS), F32)],
        2_500_000_000,
        40,
    )
    back2 = move((g2.astype(F32) + back3.astype(F32)).astype(BF16), backward(on(2)))
    back4 = move(half4, lambda i: on(-4)(returned[i]))
    back1 = move(g1, backward(on(1)))
    square = ((ROWS, 2 * HEAD), BF16)
    mine, send = call(
        finish_kernel, 0, (grad_own, back1, back2, back4), (square, square), [], 0, 16
    )
    theirs = swap(send)
    gk, gv = call(join_kernel, 1, (where, mine, theirs), (square, square), [], 0, 16)

    def joined(mine, theirs):
        return jnp.where(
            half == 0,
            jnp.concatenate([mine, theirs], axis=1),
            jnp.concatenate([theirs, mine], axis=1),
        )

    out_other, gq_other = swap(out[1]), swap(gq[1])
    out = joined(out[0], out_other)
    gq = joined(gq[0], gq_other)
    return (
        out,
        gq,
        gk,
        gv,
    )


def solution(mesh):
    rows = P(AXES, None)
    return jax.shard_map(
        per_device,
        mesh=mesh,
        in_specs=(rows, rows, rows, P(), P(), P(), rows),
        out_specs=(rows, rows, rows, rows),
        check_vma=False,
    )
```

```python
import math

import jax
import jax.numpy as jnp
from jax import lax
from jax.experimental import pallas as pl
from jax.experimental.pallas import tpu as pltpu
from jax.sharding import PartitionSpec as P


AXES = ("ctx", "grp")
ROWS = 256
HEAD = 128
GROUP = 4
HALF = GROUP * HEAD
COLS = GROUP * ROWS
SEL = 4
BLOCKS = 128
SCALE = HEAD**-0.5
SCALE_LOG2E = SCALE * math.log2(math.e)
MASKED = -1e30
FLOOR = -1e29
EPS = 1e-06

NT = (((1,), (1,)), ((), ()))
NN = (((1,), (0,)), ((), ()))
F32 = jnp.float32
BF16 = jnp.bfloat16


def dot(a, b, dims):
    return lax.dot_general(a, b, dims, preferred_element_type=F32)


def geometry(where_ref):
    me = where_ref[0]
    half = me % 2
    chip = me // 2

    def place(block):
        return 2 * (chip - block // 2) + (block % 2 + half) % 2

    return half, (me, me + 1 - 2 * half), place


def stack_heads(qs, q_ref):
    for n in range(GROUP):
        qs[n * ROWS : (n + 1) * ROWS, :] = q_ref[:, n * HEAD : (n + 1) * HEAD]


def window_scores(table, at, before, seen, queries):
    diag = dot(table[at, :, :HEAD], queries, NT)
    key_at = lax.broadcasted_iota(jnp.int32, (ROWS, COLS), 0)
    query_at = lax.broadcasted_iota(jnp.int32, (ROWS, COLS), 1) % ROWS
    diag = jnp.where(key_at <= query_at, diag, MASKED)
    prev = jnp.where(seen, dot(table[before, :, :HEAD], queries, NT), MASKED)
    return diag, prev


def load_table(table, *refs):
    for k, ref in enumerate(refs):
        for s in range(2):
            table[2 * k + s] = ref[s]


def slots_of(block, offset_ref, place):
    count = offset_ref[BLOCKS * SEL + block]
    seen, places = [], []
    for j in range(SEL):
        source = block - offset_ref[block * SEL + j]
        seen.append((source >= 0) & (j < count))
        places.append(place(jnp.maximum(source, 0)))
    return count, seen, places


def ranked(flags, values):
    number = jnp.int32(0)
    order = [jnp.int32(0)] * SEL
    for flag, value in zip(flags, values):
        for r in range(SEL):
            order[r] = jnp.where(flag & (number == r), value, order[r])
        number = number + flag.astype(jnp.int32)
    return number, order


def window_kernel(
    where_ref,
    offset_ref,
    q0_ref,
    q1_ref,
    ct0_ref,
    ct1_ref,
    gain_ref,
    kv0_ref,
    kv1_ref,
    kv2_ref,
    out_ref,
    stat_ref,
    gain_t_ref,
    normed_ref,
    near_ref,
    near_stat_ref,
    table,
    qs,
):
    half, _, place = geometry(where_ref)
    me = where_ref[0]
    load_table(table, kv0_ref, kv1_ref, kv2_ref)
    gains = gain_ref[pl.ds(half, 1), :]
    for n in range(GROUP):
        row = gains[:, n * HEAD : (n + 1) * HEAD]
        gain_t_ref[:, n * ROWS : (n + 1) * ROWS] = jnp.broadcast_to(row, (ROWS, HEAD)).T
    for i, (q_ref, ct_ref) in enumerate(((q0_ref, ct0_ref), (q1_ref, ct1_ref))):
        stack_heads(qs.at[i], q_ref)
        for n in range(GROUP):
            at = slice(n * ROWS, (n + 1) * ROWS)
            ct_t = ct_ref[:, n * HEAD : (n + 1) * HEAD].astype(F32).T
            normed_ref[i, :, at] = ct_t * gain_t_ref[:, at]

    def one_block(i, carry):
        block = me + i * (1 - 2 * half)
        at, before = place(block), place(jnp.maximum(block - 1, 0))
        diag, prev = window_scores(table, at, before, block >= 1, qs[i])
        top = jnp.maximum(
            jnp.max(diag, axis=0, keepdims=True), jnp.max(prev, axis=0, keepdims=True)
        )
        diag = jnp.exp2((diag - top) * SCALE_LOG2E)
        prev = jnp.exp2((prev - top) * SCALE_LOG2E)
        total = jnp.sum(diag, axis=0, keepdims=True) + jnp.sum(prev, axis=0, keepdims=True)
        inv = 1.0 / jnp.maximum(total, 1.0)
        out_ref[i] = dot(table[at, :, HEAD:].T, (diag * inv).astype(BF16), NN) + dot(
            table[before, :, HEAD:].T, (prev * inv).astype(BF16), NN
        )
        stat_ref[i, 0:1, :] = top
        stat_ref[i, 1:2, :] = inv

        _, seen, places = slots_of(block, offset_ref, place)
        number, spots = ranked([s & (p < 6) for s, p in zip(seen, places)], places)

        def near(slots):
            queries = qs[i]
            scores = [dot(table[spots[r], :, :HEAD], queries, NT) for r in range(slots)]
            top = jnp.full((1, COLS), FLOOR, F32)
            for s in scores:
                top = jnp.maximum(top, jnp.max(s, axis=0, keepdims=True))
            total = jnp.zeros((1, COLS), F32)
            out = jnp.zeros((HEAD, COLS), F32)
            for r, s in enumerate(scores):
                e = jnp.exp2((s - top) * SCALE_LOG2E)
                total = total + jnp.sum(e, axis=0, keepdims=True)
                out = out + dot(table[spots[r], :, HEAD:].T, e.astype(BF16), NN)
            near_ref[i] = out
            near_stat_ref[i, 0:1, :] = top
            near_stat_ref[i, 1:2, :] = total

        for slots in range(SEL + 1):
            pl.when(number == slots)(lambda slots=slots: near(slots))
        return carry

    lax.fori_loop(0, 2, one_block, 0)


def back_step(table, acc, at, to, p, queries, low, inner):
    grad_w = dot(table[at, :, HEAD:], low, NN)
    grad_s = (SCALE * p * (grad_w - inner)).astype(BF16)
    acc[to, :, HEAD:] += dot(p.astype(BF16), low, NT)
    acc[to, :, :HEAD] += dot(grad_s, queries, NN)
    return dot(table[at, :, :HEAD].T, grad_s, NN)


def chosen_kernel(
    where_ref,
    offset_ref,
    q0_ref,
    q1_ref,
    gain_t_ref,
    normed_ref,
    window_ref,
    near_ref,
    near_stat_ref,
    kv3_ref,
    kv4_ref,
    out_ref,
    low_ref,
    inner_ref,
    stat_ref,
    gq_ref,
    g3_ref,
    g4_ref,
    table,
    soft,
    acc,
    qs,
    ot,
):
    half, _, place = geometry(where_ref)
    me = where_ref[0]
    load_table(table, kv3_ref, kv4_ref)
    acc[...] = jnp.zeros_like(acc)
    stack_heads(qs.at[0], q0_ref)
    stack_heads(qs.at[1], q1_ref)

    def one_block(i, carry):
        block = me + i * (1 - 2 * half)
        _, seen, places = slots_of(block, offset_ref, place)
        number, spots = ranked([s & (p >= 6) for s, p in zip(seen, places)], places)

        def forward(slots):
            queries = qs[i]
            near_top = near_stat_ref[i, 0:1, :]
            top = near_top
            scores = []
            for r in range(slots):
                s = dot(table[spots[r] - 6, :, :HEAD], queries, NT)
                top = jnp.maximum(top, jnp.max(s, axis=0, keepdims=True))
                scores.append(s)
            alpha = jnp.exp2((near_top - top) * SCALE_LOG2E)
            total = near_stat_ref[i, 1:2, :] * alpha
            for r in range(slots):
                scores[r] = jnp.exp2((scores[r] - top) * SCALE_LOG2E)
                total = total + jnp.sum(scores[r], axis=0, keepdims=True)
            inv = 1.0 / jnp.maximum(total, 1.0)
            out = near_ref[i] * (alpha * inv)
            for r in range(slots):
                p = scores[r] * inv
                soft[r] = p
                out = out + dot(table[spots[r] - 6, :, HEAD:].T, p.astype(BF16), NN)
            ot[...] = out
            stat_ref[i, 0:1, :] = top
            stat_ref[i, 1:2, :] = inv

        for slots in range(SEL + 1):
            pl.when(number == slots)(lambda slots=slots: forward(slots))

        out_w = window_ref[i]
        out_c = ot[...]
        summed = out_w + out_c
        inverse = lax.rsqrt(jnp.mean(summed * summed, axis=0, keepdims=True) + EPS)
        normed = summed * inverse
        grad_normed = normed_ref[i]
        inner = jnp.mean(grad_normed * normed, axis=0, keepdims=True)
        low = (inverse * (grad_normed - normed * inner)).astype(BF16)
        wide = low.astype(F32)
        inner_c = jnp.sum(wide * out_c, axis=0, keepdims=True)
        inner_ref[i, 0:1, :] = jnp.sum(wide * out_w, axis=0, keepdims=True)
        inner_ref[i, 1:2, :] = inner_c
        low_ref[i] = low
        out_ref[i] = (normed * gain_t_ref[...]).astype(BF16)

        def backward(slots):
            gq = jnp.zeros((HEAD, COLS), F32)
            for r in range(slots):
                at = spots[r] - 6
                gq = gq + back_step(table, acc, at, at, soft[r], qs[i], low_ref[i], inner_c)
            gq_ref[i] = gq

        for slots in range(SEL + 1):
            pl.when(number == slots)(lambda slots=slots: backward(slots))
        return carry

    lax.fori_loop(0, 2, one_block, 0)
    g3_ref[...] = acc[0:2].astype(BF16)
    g4_ref[...] = acc[2:4].astype(BF16)


def slot_step(table, acc, spot, top, inv, queries, low, inner):
    p = jnp.exp2((dot(table[spot, :, :HEAD], queries, NT) - top) * SCALE_LOG2E) * inv
    return back_step(table, acc, spot, spot, p, queries, low, inner)


def near_kernel(
    where_ref,
    offset_ref,
    q0_ref,
    q1_ref,
    kv1_ref,
    kv2_ref,
    statw_ref,
    statc_ref,
    low_ref,
    inner_ref,
    gqf_ref,
    gq_ref,
    g1_ref,
    g2_ref,
    table,
    acc,
    qs,
):
    half, _, place = geometry(where_ref)
    me = where_ref[0]
    load_table(table, kv1_ref, kv2_ref)
    acc[...] = jnp.zeros_like(acc)
    stack_heads(qs.at[0], q0_ref)
    stack_heads(qs.at[1], q1_ref)

    def one_block(i, carry):
        block = me + i * (1 - 2 * half)
        gq_ref[i] = gqf_ref[i]

        @pl.when((block % 2 == 0) & (block >= 1))
        def _():
            gq_ref[i] += slot_step(
                table,
                acc,
                jnp.maximum(place(jnp.maximum(block - 1, 0)) - 2, 0),
                statw_ref[i, 0:1, :],
                statw_ref[i, 1:2, :],
                qs[i],
                low_ref[i],
                inner_ref[i, 0:1, :],
            )

        _, seen, places = slots_of(block, offset_ref, place)
        number, spots = ranked([s & (p < 6) for s, p in zip(seen, places)], places)

        def chosen(slots):
            queries = qs[i]
            low = low_ref[i]
            top = statc_ref[i, 0:1, :]
            inv = statc_ref[i, 1:2, :]
            inner = inner_ref[i, 1:2, :]
            gq = gq_ref[i]
            for r in range(slots):
                gq = gq + slot_step(table, acc, spots[r] - 2, top, inv, queries, low, inner)
            gq_ref[i] = gq

        for slots in range(1, SEL + 1):
            pl.when(number == slots)(lambda slots=slots: chosen(slots))
        return carry

    lax.fori_loop(0, 2, one_block, 0)
    g1_ref[...] = acc[0:2].astype(BF16)
    g2_ref[...] = acc[2:4].astype(BF16)


def own_kernel(
    where_ref,
    q0_ref,
    q1_ref,
    kv0_ref,
    statw_ref,
    low_ref,
    inner_ref,
    gqn_ref,
    gq_ref,
    own_ref,
    qs,
):
    half, _, place = geometry(where_ref)
    me = where_ref[0]
    own_ref[...] = jnp.zeros_like(own_ref)
    stack_heads(qs.at[0], q0_ref)
    stack_heads(qs.at[1], q1_ref)

    def one_block(i, carry):
        block = me + i * (1 - 2 * half)
        at = place(block)

        def window(odd):
            queries = qs[i]
            low = low_ref[i]
            top = statw_ref[i, 0:1, :]
            inv = statw_ref[i, 1:2, :]
            inner = inner_ref[i, 0:1, :]
            diag = dot(kv0_ref[at, :, :HEAD], queries, NT)
            key_at = lax.broadcasted_iota(jnp.int32, (ROWS, COLS), 0)
            query_at = lax.broadcasted_iota(jnp.int32, (ROWS, COLS), 1) % ROWS
            diag = jnp.where(key_at <= query_at, diag, MASKED)
            p = jnp.exp2((diag - top) * SCALE_LOG2E) * inv
            gq = gqn_ref[i] + back_step(kv0_ref, own_ref, at, at, p, queries, low, inner)
            if odd:
                gq = gq + slot_step(kv0_ref, own_ref, 1 - at, top, inv, queries, low, inner)
            gq_ref[i] = gq.astype(BF16)

        for odd in range(2):
            pl.when(block % 2 == odd)(lambda odd=odd: window(odd))
        return carry

    lax.fori_loop(0, 2, one_block, 0)


def finish_kernel(own_ref, a_ref, b_ref, c_ref, mine_ref, theirs_ref):
    for s, ref in enumerate((mine_ref, theirs_ref)):
        total = own_ref[s] + a_ref[s].astype(F32) + b_ref[s].astype(F32) + c_ref[s].astype(F32)
        ref[...] = total.astype(BF16)


def emit_kernel(where_ref, out0_ref, out1_ref, gq0_ref, gq1_ref, out_ref, gq_ref):
    half = where_ref[0] % 2

    def write(ref, source, side):
        for n in range(GROUP):
            at = (side * GROUP + n) * HEAD
            ref[:, at : at + HEAD] = source[:, n * ROWS : (n + 1) * ROWS].astype(F32).T.astype(BF16)

    for side in range(2):

        @pl.when(half == side)
        def _(side=side):
            write(out_ref, out0_ref, side)
            write(out_ref, out1_ref, 1 - side)
            write(gq_ref, gq0_ref, side)
            write(gq_ref, gq1_ref, 1 - side)


def join_kernel(where_ref, mine_ref, theirs_ref, gk_ref, gv_ref):
    first = where_ref[0] % 2 == 0
    for n, ref in enumerate((gk_ref, gv_ref)):
        at = slice(n * HEAD, (n + 1) * HEAD)
        mine, theirs = mine_ref[:, at], theirs_ref[:, at]
        ref[:, :HEAD] = jnp.where(first, mine, theirs)
        ref[:, HEAD:] = jnp.where(first, theirs, mine)


VMEM = pl.BlockSpec(memory_space=pltpu.VMEM)
SMEM = pl.BlockSpec(memory_space=pltpu.SMEM)
PAIR = (2, ROWS, 2 * HEAD)
WIDE = (2, HEAD, COLS)


def table_of(blocks, dtype):
    return pltpu.VMEM((blocks, ROWS, 2 * HEAD), dtype)


def call(kernel, scalars, args, outs, scratch, flops, limit):
    return pl.pallas_call(
        kernel,
        out_shape=[jax.ShapeDtypeStruct(*out) for out in outs],
        in_specs=[SMEM] * scalars + [VMEM] * (len(args) - scalars),
        out_specs=[VMEM] * len(outs),
        scratch_shapes=scratch,
        compiler_params=pltpu.CompilerParams(vmem_limit_bytes=limit << 20),
        cost_estimate=pl.CostEstimate(flops=flops, bytes_accessed=4_000_000, transcendentals=0),
    )(*args)


def per_device(queries, key_rows, value_rows, chosen_offset, chosen_count, head_gain, cotangent):
    size = lax.axis_size(AXES)
    groups = lax.axis_size("grp")
    side = 4
    me = lax.axis_index(AXES)
    half = me % 2

    def move(x, target):
        return lax.ppermute(x, AXES, [(i, target(i)) for i in range(size)])

    def swap(x):
        return move(x, lambda i: i ^ 1)

    def on(k):
        return lambda i: (i + 2 * k) % size

    def relay(i):
        ctx, grp = divmod(i, groups)
        top, x, y = ctx // side**2, ctx // side % side, ctx % side
        top = top ^ int(x == side - 1 and y >= side - 2)
        return ((top * side + x) * side + (y - 1) % side) * groups + grp

    def relay_back(i):
        ctx, grp = divmod(i, groups)
        top, x, y = ctx // side**2, ctx // side % side, ctx % side
        top = top ^ int(x == 0 and y < 2)
        return ((top * side + x) * side + (y + 1) % side) * groups + grp

    relayed = {relay(i): i for i in range(size)}
    returned = {relay_back(i): i for i in range(size)}

    def onward(i):
        return on(4)(relayed[i])

    def backward(target):
        from_ = {target(i): i for i in range(size)}
        return lambda i: from_[i]

    def part(x, which, width):
        return lax.dynamic_slice(x, (0, which * width), (x.shape[0], width))

    def head_of(which):
        return jnp.concatenate([part(key_rows, which, HEAD), part(value_rows, which, HEAD)], axis=1)

    other = 1 - half
    own = jnp.stack([head_of(half), swap(head_of(other))])
    kv2 = move(own, on(2))
    half4 = move(own, relay)
    kv1 = move(own, on(1))
    kv3 = move(kv2, on(1))
    kv4 = move(half4, onward)

    where = me.astype(jnp.int32).reshape(1)
    q0, q1 = part(queries, half, HALF), swap(part(queries, other, HALF))
    ct0, ct1 = part(cotangent, half, HALF), swap(part(cotangent, other, HALF))
    stat = ((2, 2, COLS), F32)
    offsets = jnp.concatenate([chosen_offset.reshape(-1), chosen_count])
    queues = pltpu.VMEM((2, COLS, HEAD), BF16)
    window, window_stats, gain_t, normed, near, near_stats = call(
        window_kernel,
        2,
        (where, offsets, q0, q1, ct0, ct1, head_gain.reshape(2, HALF), own, kv1, kv2),
        ((WIDE, F32), stat, ((HEAD, COLS), F32), (WIDE, F32), (WIDE, F32), stat),
        [table_of(6, BF16), queues],
        800_000_000,
        32,
    )
    out, low, inner, chosen_stats, gq_far, g3, g4 = call(
        chosen_kernel,
        2,
        (where, offsets, q0, q1, gain_t, normed, window, near, near_stats, kv3, kv4),
        ((WIDE, BF16), (WIDE, BF16), stat, stat, (WIDE, F32), (PAIR, BF16), (PAIR, BF16)),
        [
            table_of(4, BF16),
            pltpu.VMEM((SEL, ROWS, COLS), F32),
            table_of(4, F32),
            queues,
            pltpu.VMEM((HEAD, COLS), F32),
        ],
        2_500_000_000,
        40,
    )
    back3 = move(g3, backward(on(1)))
    half4 = move(g4, relay_back)
    gq_near, g1, g2 = call(
        near_kernel,
        2,
        (where, offsets, q0, q1, kv1, kv2, window_stats, chosen_stats, low, inner, gq_far),
        ((WIDE, F32), (PAIR, BF16), (PAIR, BF16)),
        [table_of(4, BF16), table_of(4, F32), queues],
        2_000_000_000,
        40,
    )
    gq, grad_own = call(
        own_kernel,
        1,
        (where, q0, q1, own, window_stats, low, inner, gq_near),
        ((WIDE, BF16), (PAIR, F32)),
        [queues],
        1_500_000_000,
        40,
    )
    back2 = move((g2.astype(F32) + back3.astype(F32)).astype(BF16), backward(on(2)))
    back4 = move(half4, lambda i: on(-4)(returned[i]))
    back1 = move(g1, backward(on(1)))
    square = ((ROWS, 2 * HEAD), BF16)
    mine, send = call(
        finish_kernel, 0, (grad_own, back1, back2, back4), (square, square), [], 0, 16
    )
    theirs = swap(send)
    gk, gv = call(join_kernel, 1, (where, mine, theirs), (square, square), [], 0, 16)

    out_other, gq_other = swap(out[1]), swap(gq[1])
    full = ((ROWS, 2 * HALF), BF16)
    out, gq = call(
        emit_kernel, 1, (where, out[0], out_other, gq[0], gq_other), (full, full), [], 0, 16
    )
    return (
        out,
        gq,
        gk,
        gv,
    )


def solution(mesh):
    rows = P(AXES, None)
    return jax.shard_map(
        per_device,
        mesh=mesh,
        in_specs=(rows, rows, rows, P(), P(), P(), rows),
        out_specs=(rows, rows, rows, rows),
        check_vma=False,
    )
```

```python
import math

import jax
import jax.numpy as jnp
from jax import lax
from jax.experimental import pallas as pl
from jax.experimental.pallas import tpu as pltpu
from jax.sharding import PartitionSpec as P


AXES = ("ctx", "grp")
ROWS = 256
HEAD = 128
GROUP = 4
HALF = GROUP * HEAD
COLS = GROUP * ROWS
SEL = 4
BLOCKS = 128
SCALE = HEAD**-0.5
SCALE_LOG2E = SCALE * math.log2(math.e)
MASKED = -1e30
FLOOR = -1e29
EPS = 1e-06

NT = (((1,), (1,)), ((), ()))
NN = (((1,), (0,)), ((), ()))
F32 = jnp.float32
BF16 = jnp.bfloat16


def dot(a, b, dims):
    return lax.dot_general(a, b, dims, preferred_element_type=F32)


def geometry(where_ref):
    me = where_ref[0]
    half = me % 2
    chip = me // 2

    def place(block):
        return 2 * (chip - block // 2) + (block % 2 + half) % 2

    return half, (me, me + 1 - 2 * half), place


def stack_heads(qs, q_ref):
    for n in range(GROUP):
        qs[n * ROWS : (n + 1) * ROWS, :] = q_ref[:, n * HEAD : (n + 1) * HEAD]


def window_scores(table, at, before, seen, queries):
    diag = dot(table[at, :, :HEAD], queries, NT)
    key_at = lax.broadcasted_iota(jnp.int32, (ROWS, COLS), 0)
    query_at = lax.broadcasted_iota(jnp.int32, (ROWS, COLS), 1) % ROWS
    diag = jnp.where(key_at <= query_at, diag, MASKED)
    prev = jnp.where(seen, dot(table[before, :, :HEAD], queries, NT), MASKED)
    return diag, prev


def load_table(table, *refs):
    for k, ref in enumerate(refs):
        for s in range(2):
            table[2 * k + s] = ref[s]


def slots_of(block, offset_ref, place):
    count = offset_ref[BLOCKS * SEL + block]
    seen, places = [], []
    for j in range(SEL):
        source = block - offset_ref[block * SEL + j]
        seen.append((source >= 0) & (j < count))
        places.append(place(jnp.maximum(source, 0)))
    return count, seen, places


def ranked(flags, values):
    number = jnp.int32(0)
    order = [jnp.int32(0)] * SEL
    for flag, value in zip(flags, values):
        for r in range(SEL):
            order[r] = jnp.where(flag & (number == r), value, order[r])
        number = number + flag.astype(jnp.int32)
    return number, order


def window_kernel(
    where_ref,
    offset_ref,
    q0_ref,
    q1_ref,
    ct0_ref,
    ct1_ref,
    gain_ref,
    kv0_ref,
    kv1_ref,
    kv2_ref,
    out_ref,
    stat_ref,
    gain_t_ref,
    normed_ref,
    near_ref,
    near_stat_ref,
    qs,
    table,
):
    half, _, place = geometry(where_ref)
    me = where_ref[0]
    load_table(table, kv0_ref, kv1_ref, kv2_ref)
    gains = gain_ref[pl.ds(half, 1), :]
    for n in range(GROUP):
        row = gains[:, n * HEAD : (n + 1) * HEAD]
        gain_t_ref[:, n * ROWS : (n + 1) * ROWS] = jnp.broadcast_to(row, (ROWS, HEAD)).T
    for i, (q_ref, ct_ref) in enumerate(((q0_ref, ct0_ref), (q1_ref, ct1_ref))):
        stack_heads(qs.at[i], q_ref)
        for n in range(GROUP):
            at = slice(n * ROWS, (n + 1) * ROWS)
            ct_t = ct_ref[:, n * HEAD : (n + 1) * HEAD].astype(F32).T
            normed_ref[i, :, at] = ct_t * gain_t_ref[:, at]

    def one_block(i, carry):
        block = me + i * (1 - 2 * half)
        at, before = place(block), place(jnp.maximum(block - 1, 0))
        diag, prev = window_scores(table, at, before, block >= 1, qs[i])
        top = jnp.maximum(
            jnp.max(diag, axis=0, keepdims=True), jnp.max(prev, axis=0, keepdims=True)
        )
        diag = jnp.exp2((diag - top) * SCALE_LOG2E)
        prev = jnp.exp2((prev - top) * SCALE_LOG2E)
        total = jnp.sum(diag, axis=0, keepdims=True) + jnp.sum(prev, axis=0, keepdims=True)
        inv = 1.0 / jnp.maximum(total, 1.0)
        out_ref[i] = dot(table[at, :, HEAD:].T, (diag * inv).astype(BF16), NN) + dot(
            table[before, :, HEAD:].T, (prev * inv).astype(BF16), NN
        )
        stat_ref[i, 0:1, :] = top
        stat_ref[i, 1:2, :] = inv

        _, seen, places = slots_of(block, offset_ref, place)
        number, spots = ranked([s & (p < 6) for s, p in zip(seen, places)], places)

        def near(slots):
            queries = qs[i]
            scores = [dot(table[spots[r], :, :HEAD], queries, NT) for r in range(slots)]
            top = jnp.full((1, COLS), FLOOR, F32)
            for s in scores:
                top = jnp.maximum(top, jnp.max(s, axis=0, keepdims=True))
            total = jnp.zeros((1, COLS), F32)
            out = jnp.zeros((HEAD, COLS), F32)
            for r, s in enumerate(scores):
                e = jnp.exp2((s - top) * SCALE_LOG2E)
                total = total + jnp.sum(e, axis=0, keepdims=True)
                out = out + dot(table[spots[r], :, HEAD:].T, e.astype(BF16), NN)
            near_ref[i] = out
            near_stat_ref[i, 0:1, :] = top
            near_stat_ref[i, 1:2, :] = total

        for slots in range(SEL + 1):
            pl.when(number == slots)(lambda slots=slots: near(slots))
        return carry

    lax.fori_loop(0, 2, one_block, 0)


def back_step(table, acc, at, to, p, queries, low, inner):
    grad_w = dot(table[at, :, HEAD:], low, NN)
    grad_s = (SCALE * p * (grad_w - inner)).astype(BF16)
    acc[to, :, HEAD:] += dot(p.astype(BF16), low, NT)
    acc[to, :, :HEAD] += dot(grad_s, queries, NN)
    return dot(table[at, :, :HEAD].T, grad_s, NN)


def chosen_kernel(
    where_ref,
    offset_ref,
    qs,
    gain_t_ref,
    normed_ref,
    window_ref,
    near_ref,
    near_stat_ref,
    kv3_ref,
    kv4_ref,
    out_ref,
    low_ref,
    inner_ref,
    stat_ref,
    gq_ref,
    g3_ref,
    g4_ref,
    table,
    soft,
    acc,
    ot,
):
    half, _, place = geometry(where_ref)
    me = where_ref[0]
    load_table(table, kv3_ref, kv4_ref)
    acc[...] = jnp.zeros_like(acc)

    def one_block(i, carry):
        block = me + i * (1 - 2 * half)
        _, seen, places = slots_of(block, offset_ref, place)
        number, spots = ranked([s & (p >= 6) for s, p in zip(seen, places)], places)

        def forward(slots):
            queries = qs[i]
            near_top = near_stat_ref[i, 0:1, :]
            top = near_top
            scores = []
            for r in range(slots):
                s = dot(table[spots[r] - 6, :, :HEAD], queries, NT)
                top = jnp.maximum(top, jnp.max(s, axis=0, keepdims=True))
                scores.append(s)
            alpha = jnp.exp2((near_top - top) * SCALE_LOG2E)
            total = near_stat_ref[i, 1:2, :] * alpha
            for r in range(slots):
                scores[r] = jnp.exp2((scores[r] - top) * SCALE_LOG2E)
                total = total + jnp.sum(scores[r], axis=0, keepdims=True)
            inv = 1.0 / jnp.maximum(total, 1.0)
            out = near_ref[i] * (alpha * inv)
            for r in range(slots):
                p = scores[r] * inv
                soft[r] = p
                out = out + dot(table[spots[r] - 6, :, HEAD:].T, p.astype(BF16), NN)
            ot[...] = out
            stat_ref[i, 0:1, :] = top
            stat_ref[i, 1:2, :] = inv

        for slots in range(SEL + 1):
            pl.when(number == slots)(lambda slots=slots: forward(slots))

        out_w = window_ref[i]
        out_c = ot[...]
        summed = out_w + out_c
        inverse = lax.rsqrt(jnp.mean(summed * summed, axis=0, keepdims=True) + EPS)
        normed = summed * inverse
        grad_normed = normed_ref[i]
        inner = jnp.mean(grad_normed * normed, axis=0, keepdims=True)
        low = (inverse * (grad_normed - normed * inner)).astype(BF16)
        wide = low.astype(F32)
        inner_c = jnp.sum(wide * out_c, axis=0, keepdims=True)
        inner_ref[i, 0:1, :] = jnp.sum(wide * out_w, axis=0, keepdims=True)
        inner_ref[i, 1:2, :] = inner_c
        low_ref[i] = low
        out_ref[i] = (normed * gain_t_ref[...]).astype(BF16)

        def backward(slots):
            gq = jnp.zeros((HEAD, COLS), F32)
            for r in range(slots):
                at = spots[r] - 6
                gq = gq + back_step(table, acc, at, at, soft[r], qs[i], low_ref[i], inner_c)
            gq_ref[i] = gq

        for slots in range(SEL + 1):
            pl.when(number == slots)(lambda slots=slots: backward(slots))
        return carry

    lax.fori_loop(0, 2, one_block, 0)
    g3_ref[...] = acc[0:2].astype(BF16)
    g4_ref[...] = acc[2:4].astype(BF16)


def slot_step(table, acc, spot, top, inv, queries, low, inner):
    p = jnp.exp2((dot(table[spot, :, :HEAD], queries, NT) - top) * SCALE_LOG2E) * inv
    return back_step(table, acc, spot, spot, p, queries, low, inner)


def near_kernel(
    where_ref,
    offset_ref,
    qs,
    kv1_ref,
    kv2_ref,
    statw_ref,
    statc_ref,
    low_ref,
    inner_ref,
    gqf_ref,
    gq_ref,
    g1_ref,
    g2_ref,
    table,
    acc,
):
    half, _, place = geometry(where_ref)
    me = where_ref[0]
    load_table(table, kv1_ref, kv2_ref)
    acc[...] = jnp.zeros_like(acc)

    def one_block(i, carry):
        block = me + i * (1 - 2 * half)
        gq_ref[i] = gqf_ref[i]

        @pl.when((block % 2 == 0) & (block >= 1))
        def _():
            gq_ref[i] += slot_step(
                table,
                acc,
                jnp.maximum(place(jnp.maximum(block - 1, 0)) - 2, 0),
                statw_ref[i, 0:1, :],
                statw_ref[i, 1:2, :],
                qs[i],
                low_ref[i],
                inner_ref[i, 0:1, :],
            )

        _, seen, places = slots_of(block, offset_ref, place)
        number, spots = ranked([s & (p < 6) for s, p in zip(seen, places)], places)

        def chosen(slots):
            queries = qs[i]
            low = low_ref[i]
            top = statc_ref[i, 0:1, :]
            inv = statc_ref[i, 1:2, :]
            inner = inner_ref[i, 1:2, :]
            gq = gq_ref[i]
            for r in range(slots):
                gq = gq + slot_step(table, acc, spots[r] - 2, top, inv, queries, low, inner)
            gq_ref[i] = gq

        for slots in range(1, SEL + 1):
            pl.when(number == slots)(lambda slots=slots: chosen(slots))
        return carry

    lax.fori_loop(0, 2, one_block, 0)
    g1_ref[...] = acc[0:2].astype(BF16)
    g2_ref[...] = acc[2:4].astype(BF16)


def own_kernel(
    where_ref,
    qs,
    kv0_ref,
    statw_ref,
    low_ref,
    inner_ref,
    gqn_ref,
    gq_ref,
    own_ref,
):
    half, _, place = geometry(where_ref)
    me = where_ref[0]
    own_ref[...] = jnp.zeros_like(own_ref)

    def one_block(i, carry):
        block = me + i * (1 - 2 * half)
        at = place(block)

        def window(odd):
            queries = qs[i]
            low = low_ref[i]
            top = statw_ref[i, 0:1, :]
            inv = statw_ref[i, 1:2, :]
            inner = inner_ref[i, 0:1, :]
            diag = dot(kv0_ref[at, :, :HEAD], queries, NT)
            key_at = lax.broadcasted_iota(jnp.int32, (ROWS, COLS), 0)
            query_at = lax.broadcasted_iota(jnp.int32, (ROWS, COLS), 1) % ROWS
            diag = jnp.where(key_at <= query_at, diag, MASKED)
            p = jnp.exp2((diag - top) * SCALE_LOG2E) * inv
            gq = gqn_ref[i] + back_step(kv0_ref, own_ref, at, at, p, queries, low, inner)
            if odd:
                gq = gq + slot_step(kv0_ref, own_ref, 1 - at, top, inv, queries, low, inner)
            gq_ref[i] = gq.astype(BF16)

        for odd in range(2):
            pl.when(block % 2 == odd)(lambda odd=odd: window(odd))
        return carry

    lax.fori_loop(0, 2, one_block, 0)


def finish_kernel(own_ref, a_ref, b_ref, c_ref, mine_ref, theirs_ref):
    for s, ref in enumerate((mine_ref, theirs_ref)):
        total = own_ref[s] + a_ref[s].astype(F32) + b_ref[s].astype(F32) + c_ref[s].astype(F32)
        ref[...] = total.astype(BF16)


def emit_kernel(where_ref, out0_ref, out1_ref, gq0_ref, gq1_ref, out_ref, gq_ref):
    half = where_ref[0] % 2

    def write(ref, source, side):
        for n in range(GROUP):
            at = (side * GROUP + n) * HEAD
            ref[:, at : at + HEAD] = source[:, n * ROWS : (n + 1) * ROWS].astype(F32).T.astype(BF16)

    for side in range(2):

        @pl.when(half == side)
        def _(side=side):
            write(out_ref, out0_ref, side)
            write(out_ref, out1_ref, 1 - side)
            write(gq_ref, gq0_ref, side)
            write(gq_ref, gq1_ref, 1 - side)


def join_kernel(where_ref, mine_ref, theirs_ref, gk_ref, gv_ref):
    first = where_ref[0] % 2 == 0
    for n, ref in enumerate((gk_ref, gv_ref)):
        at = slice(n * HEAD, (n + 1) * HEAD)
        mine, theirs = mine_ref[:, at], theirs_ref[:, at]
        ref[:, :HEAD] = jnp.where(first, mine, theirs)
        ref[:, HEAD:] = jnp.where(first, theirs, mine)


VMEM = pl.BlockSpec(memory_space=pltpu.VMEM)
SMEM = pl.BlockSpec(memory_space=pltpu.SMEM)
PAIR = (2, ROWS, 2 * HEAD)
WIDE = (2, HEAD, COLS)


def table_of(blocks, dtype):
    return pltpu.VMEM((blocks, ROWS, 2 * HEAD), dtype)


def call(kernel, scalars, args, outs, scratch, flops, limit):
    return pl.pallas_call(
        kernel,
        out_shape=[jax.ShapeDtypeStruct(*out) for out in outs],
        in_specs=[SMEM] * scalars + [VMEM] * (len(args) - scalars),
        out_specs=[VMEM] * len(outs),
        scratch_shapes=scratch,
        compiler_params=pltpu.CompilerParams(vmem_limit_bytes=limit << 20),
        cost_estimate=pl.CostEstimate(flops=flops, bytes_accessed=4_000_000, transcendentals=0),
    )(*args)


def per_device(queries, key_rows, value_rows, chosen_offset, chosen_count, head_gain, cotangent):
    size = lax.axis_size(AXES)
    groups = lax.axis_size("grp")
    side = 4
    me = lax.axis_index(AXES)
    half = me % 2

    def move(x, target):
        return lax.ppermute(x, AXES, [(i, target(i)) for i in range(size)])

    def swap(x):
        return move(x, lambda i: i ^ 1)

    def on(k):
        return lambda i: (i + 2 * k) % size

    def relay(i):
        ctx, grp = divmod(i, groups)
        top, x, y = ctx // side**2, ctx // side % side, ctx % side
        top = top ^ int(x == side - 1 and y >= side - 2)
        return ((top * side + x) * side + (y - 1) % side) * groups + grp

    def relay_back(i):
        ctx, grp = divmod(i, groups)
        top, x, y = ctx // side**2, ctx // side % side, ctx % side
        top = top ^ int(x == 0 and y < 2)
        return ((top * side + x) * side + (y + 1) % side) * groups + grp

    relayed = {relay(i): i for i in range(size)}
    returned = {relay_back(i): i for i in range(size)}

    def onward(i):
        return on(4)(relayed[i])

    def backward(target):
        from_ = {target(i): i for i in range(size)}
        return lambda i: from_[i]

    def part(x, which, width):
        return lax.dynamic_slice(x, (0, which * width), (x.shape[0], width))

    def head_of(which):
        return jnp.concatenate([part(key_rows, which, HEAD), part(value_rows, which, HEAD)], axis=1)

    other = 1 - half
    own = jnp.stack([head_of(half), swap(head_of(other))])
    kv2 = move(own, on(2))
    half4 = move(own, relay)
    kv1 = move(own, on(1))
    kv3 = move(kv2, on(1))
    kv4 = move(half4, onward)

    where = me.astype(jnp.int32).reshape(1)
    q0, q1 = part(queries, half, HALF), swap(part(queries, other, HALF))
    ct0, ct1 = part(cotangent, half, HALF), swap(part(cotangent, other, HALF))
    stat = ((2, 2, COLS), F32)
    offsets = jnp.concatenate([chosen_offset.reshape(-1), chosen_count])
    queue = ((2, COLS, HEAD), BF16)
    window, window_stats, gain_t, normed, near, near_stats, stacked = call(
        window_kernel,
        2,
        (where, offsets, q0, q1, ct0, ct1, head_gain.reshape(2, HALF), own, kv1, kv2),
        ((WIDE, F32), stat, ((HEAD, COLS), F32), (WIDE, F32), (WIDE, F32), stat, queue),
        [table_of(6, BF16)],
        800_000_000,
        32,
    )
    out, low, inner, chosen_stats, gq_far, g3, g4 = call(
        chosen_kernel,
        2,
        (where, offsets, stacked, gain_t, normed, window, near, near_stats, kv3, kv4),
        ((WIDE, BF16), (WIDE, BF16), stat, stat, (WIDE, F32), (PAIR, BF16), (PAIR, BF16)),
        [
            table_of(4, BF16),
            pltpu.VMEM((SEL, ROWS, COLS), F32),
            table_of(4, F32),
            pltpu.VMEM((HEAD, COLS), F32),
        ],
        2_500_000_000,
        40,
    )
    back3 = move(g3, backward(on(1)))
    half4 = move(g4, relay_back)
    gq_near, g1, g2 = call(
        near_kernel,
        2,
        (where, offsets, stacked, kv1, kv2, window_stats, chosen_stats, low, inner, gq_far),
        ((WIDE, F32), (PAIR, BF16), (PAIR, BF16)),
        [table_of(4, BF16), table_of(4, F32)],
        2_000_000_000,
        40,
    )
    gq, grad_own = call(
        own_kernel,
        1,
        (where, stacked, own, window_stats, low, inner, gq_near),
        ((WIDE, BF16), (PAIR, F32)),
        [],
        1_500_000_000,
        40,
    )
    back2 = move((g2.astype(F32) + back3.astype(F32)).astype(BF16), backward(on(2)))
    back4 = move(half4, lambda i: on(-4)(returned[i]))
    back1 = move(g1, backward(on(1)))
    square = ((ROWS, 2 * HEAD), BF16)
    mine, send = call(
        finish_kernel, 0, (grad_own, back1, back2, back4), (square, square), [], 0, 16
    )
    theirs = swap(send)
    gk, gv = call(join_kernel, 1, (where, mine, theirs), (square, square), [], 0, 16)

    out_other, gq_other = swap(out[1]), swap(gq[1])
    full = ((ROWS, 2 * HALF), BF16)
    out, gq = call(
        emit_kernel, 1, (where, out[0], out_other, gq[0], gq_other), (full, full), [], 0, 16
    )
    return (
        out,
        gq,
        gk,
        gv,
    )


def solution(mesh):
    rows = P(AXES, None)
    return jax.shard_map(
        per_device,
        mesh=mesh,
        in_specs=(rows, rows, rows, P(), P(), P(), rows),
        out_specs=(rows, rows, rows, rows),
        check_vma=False,
    )
```
